128 devices in a mesh: row: 8 (over z, core), col: 16 (over y, x).
Axes of the slice: x: 4, y: 4, z: 4, core: 2. Of those that a mesh axis runs over, the one named last changes fastest.
Arguments:
- video_scores_in: float32 [131072, 128], P(('col', 'row')), may hold values from -6 to 6
- audio_seed: int32 [131072], P(('row', 'col')), may hold values from 0 to 255
- video_seed: int32 [131072], P(('col', 'row')), may hold values from 0 to 255
- tile_values: bfloat16 [8, 16, 640, 128, 128], P('row', 'col'), may hold values from 0 to 1
- tile_rows: int32 [8, 16, 640], P('row', 'col'), may hold values from 0 to 127, as said below
- tile_cols: int32 [8, 16, 640], P('row', 'col'), may hold values from 0 to 63, as said below
- tile_count: int32 [8, 16], P('row', 'col'), may hold values from 128 to 640, as said below
Outputs:
- audio_scores: float32 [131072, 128], P(('row', 'col'))
- video_scores: float32 [131072, 128], P(('col', 'row'))
The draws below stay inside these ranges and needn't reach their ends.
Inputs may be any that keep to these rules, and one draw needn't show every extreme that they name: `tile_rows`: every tile row of a cell's row group and every tile column of its column group is named by some live slot of that cell; two slots may name the same tile position, and then both add. `tile_cols`: see tile_rows. `tile_count`: loads differ widely between cells; some cell uses all 640 slots.
All inputs are finite; a program needn't handle non-finite values.
Results may differ from the reference program's by a relative error of at most 0.005.
Values may be sent and summed in bfloat16 or wider, within the bound.
A program may use at most 192 MiB of HBM per device.

```python
import jax
import jax.numpy as jnp
from jax import lax

CLASSES = 128
TILE = 128
TILE_ROWS = 128
TILE_COLS = 64
TILES_DEV = 640
CLIPS = 131072
N_ROW = 8
N_COL = 16


def tile_layout(key):
    shape_slots = (N_ROW, N_COL, TILES_DEV)
    slot = jnp.arange(TILES_DEV, dtype=jnp.int32)[None, None, :]
    offset_rows = jax.random.randint(jax.random.fold_in(key, 11), (N_ROW, N_COL, 1), 0, TILE_ROWS, dtype=jnp.int32)
    offset_cols = jax.random.randint(jax.random.fold_in(key, 12), (N_ROW, N_COL, 1), 0, TILE_COLS, dtype=jnp.int32)
    random_rows = jax.random.randint(jax.random.fold_in(key, 13), shape_slots, 0, TILE_ROWS, dtype=jnp.int32)
    random_cols = jax.random.randint(jax.random.fold_in(key, 14), shape_slots, 0, TILE_COLS, dtype=jnp.int32)
    covering = slot < TILE_ROWS
    row_ids = jnp.where(covering, (slot + offset_rows) % TILE_ROWS, random_rows)
    col_ids = jnp.where(covering, (slot + offset_cols) % TILE_COLS, random_cols)
    spare = TILES_DEV - TILE_ROWS
    first = jax.random.randint(jax.random.fold_in(key, 15), (N_ROW, N_COL), 0, spare + 1, dtype=jnp.int32)
    second = jax.random.randint(jax.random.fold_in(key, 16), (N_ROW, N_COL), 0, spare + 1, dtype=jnp.int32)
    extra = first * second // spare
    order = jax.random.permutation(jax.random.fold_in(key, 17), N_ROW * N_COL).astype(jnp.int32).reshape(N_ROW, N_COL)
    extra = jnp.where(order == 0, spare, extra)
    return (row_ids, col_ids, TILE_ROWS + extra)


def draw_tile_rows(key, part):
    return tile_layout(key)[0]


def draw_tile_cols(key, part):
    return tile_layout(key)[1]


def draw_tile_count(key, part):
    return tile_layout(key)[2]


def with_ends(result, stream_key, low, high):
    extent = result.shape
    place = [jax.random.randint(jax.random.fold_in(stream_key, axis), (), 0, extent[axis]) for axis in range(len(extent))]
    result = result.at[tuple(place)].set(low)
    longest = extent.index(max(extent))
    place[longest] = (place[longest] + 1) % extent[longest]
    return result.at[tuple(place)].set(high)


def steps_of(own_key, shape, cuts, least, high):
    factor_of, own = 1.0, jax.random.fold_in(own_key, 6)
    for position, blocks in cuts:
        steps = jnp.exp(jax.random.uniform(jax.random.fold_in(own, position), (blocks,), jnp.float32, least / len(cuts), high / len(cuts)))
        factor_of = factor_of * jnp.repeat(steps, shape[position] // blocks).reshape([-1 if axis == position else 1 for axis in range(len(shape))])
    return factor_of


def scatter_about(stream_key, dims, deviation, bound, shards=(), kind=jnp.bfloat16):
    level = steps_of(stream_key, dims, shards, -0.22, 0.18) if shards else 1.0
    entries = jax.random.normal(stream_key, dims, jnp.float32) * deviation * level
    return jnp.minimum(jnp.maximum(entries, -bound), bound).astype(kind)


def setup_inputs(seed: int = 0) -> dict:
    key_list = jax.random.split(jax.random.key(seed), 8)
    video_scores_in = scatter_about(key_list[0], (CLIPS, CLASSES), 1.0, 6.0, ((0, 128),), jnp.float32)
    audio_seed = with_ends(jax.random.randint(key_list[1], (CLIPS,), 0, 2 * CLASSES), jax.random.fold_in(key_list[1], 1), 0, (2 * CLASSES) - 1).astype(jnp.int32)
    video_seed = with_ends(jax.random.randint(key_list[2], (CLIPS,), 0, 2 * CLASSES), jax.random.fold_in(key_list[2], 1), 0, (2 * CLASSES) - 1).astype(jnp.int32)
    tile_values = jnp.clip(1.0 * jax.random.uniform(key_list[3], (N_ROW, N_COL, TILES_DEV, TILE, TILE), jnp.float32) ** steps_of(key_list[3], (N_ROW, N_COL, TILES_DEV, TILE, TILE), ((0, 8), (1, 16)), -0.2, 0.2), 0.0, 1.0).astype(jnp.bfloat16)
    tile_rows = draw_tile_rows(jax.random.fold_in(key_list[7], 71), 0)
    tile_cols = draw_tile_cols(jax.random.fold_in(key_list[7], 71), 0)
    tile_count = draw_tile_count(jax.random.fold_in(key_list[7], 71), 0)
    return dict(video_scores_in=video_scores_in, audio_seed=audio_seed, video_seed=video_seed, tile_values=tile_values, tile_rows=tile_rows, tile_cols=tile_cols, tile_count=tile_count)


blend_weight = 0.75

def blend(total, masses, seed_ids):
    labels = (seed_ids[:, None] == jnp.arange(CLASSES, dtype=jnp.int32)[None, :]).astype(jnp.float32)
    return blend_weight * total / jnp.sqrt(masses)[:, None] + (1.0 - blend_weight) * labels

def reference(video_scores_in, audio_seed, video_seed, tile_values, tile_rows, tile_cols, tile_count):
    cells = N_ROW * N_COL
    flat_vals = tile_values.reshape(cells, TILES_DEV, TILE, TILE)
    flat_rows = tile_rows.reshape(cells, TILES_DEV).astype(jnp.int32)
    flat_cols = tile_cols.reshape(cells, TILES_DEV).astype(jnp.int32)
    flat_count = tile_count.reshape(cells).astype(jnp.int32)
    cell_index = jnp.arange(cells, dtype=jnp.int32)
    row_of = cell_index // N_COL
    col_of = cell_index % N_COL
    slot_index = jnp.arange(TILES_DEV, dtype=jnp.int32)
    video_half = video_scores_in.astype(jnp.bfloat16).reshape(N_COL, TILE_COLS, TILE, CLASSES)

    def forward(state, inputs):
        prop_sum, prop_mass = state
        cell_vals, cell_rows, cell_cols, cell_count, which_row, which_col = inputs
        active_flags = (slot_index < cell_count).astype(jnp.float32)
        panel_tiles = lax.dynamic_index_in_dim(video_half, which_col, 0, keepdims=False)
        selected_entries = jnp.take(panel_tiles, cell_cols, axis=0).astype(jnp.float32)
        edge_weight_list = cell_vals.astype(jnp.float32)
        weighted_products = jnp.einsum('efr,erj->efj', edge_weight_list, selected_entries) * active_flags[:, None, None]
        masses = lax.optimization_barrier(jnp.sum(edge_weight_list, axis=2)) * active_flags[:, None]
        add_sum = jax.ops.segment_sum(weighted_products, cell_rows, num_segments=TILE_ROWS)
        accumulate_mass = jax.ops.segment_sum(masses, cell_rows, num_segments=TILE_ROWS)
        return ((prop_sum.at[which_row].add(add_sum), prop_mass.at[which_row].add(accumulate_mass)), None)
    start = (jnp.zeros((N_ROW, TILE_ROWS, TILE, CLASSES), jnp.float32), jnp.zeros((N_ROW, TILE_ROWS, TILE), jnp.float32))
    (prop_sum, prop_mass), _ = lax.scan(forward, start, (flat_vals, flat_rows, flat_cols, flat_count, row_of, col_of))
    audio_scores = blend(prop_sum.reshape(CLIPS, CLASSES), prop_mass.reshape(CLIPS), audio_seed)
    audio_half = audio_scores.astype(jnp.bfloat16).reshape(N_ROW, TILE_ROWS, TILE, CLASSES)

    def backward(state, inputs):
        back_sum, back_mass = state
        cell_vals, cell_rows, cell_cols, cell_count, which_row, which_col = inputs
        active_flags = (slot_index < cell_count).astype(jnp.float32)
        panel_tiles = lax.dynamic_index_in_dim(audio_half, which_row, 0, keepdims=False)
        selected_entries = jnp.take(panel_tiles, cell_rows, axis=0).astype(jnp.float32)
        edge_weight_list = cell_vals.astype(jnp.float32)
        weighted_products = jnp.einsum('nhv,nhk->nvk', edge_weight_list, selected_entries) * active_flags[:, None, None]
        masses = lax.optimization_barrier(jnp.sum(edge_weight_list, axis=1)) * active_flags[:, None]
        add_sum = jax.ops.segment_sum(weighted_products, cell_cols, num_segments=TILE_COLS)
        accumulate_mass = jax.ops.segment_sum(masses, cell_cols, num_segments=TILE_COLS)
        return ((back_sum.at[which_col].add(add_sum), back_mass.at[which_col].add(accumulate_mass)), None)
    reverse_begin = (jnp.zeros((N_COL, TILE_COLS, TILE, CLASSES), jnp.float32), jnp.zeros((N_COL, TILE_COLS, TILE), jnp.float32))
    (back_sum, back_mass), _ = lax.scan(backward, reverse_begin, (flat_vals, flat_rows, flat_cols, flat_count, row_of, col_of))
    video_scores = blend(back_sum.reshape(CLIPS, CLASSES), back_mass.reshape(CLIPS), video_seed)
    return (audio_scores, video_scores)
```

```python
import functools

import jax
import jax.numpy as jnp
from jax import lax
from jax.experimental import pallas as pl
from jax.experimental.pallas import tpu as pltpu
from jax.sharding import PartitionSpec as P

MESH = pl.DeviceIdType.MESH
F32, BF16 = jnp.float32, jnp.bfloat16
VM = pl.BlockSpec(memory_space=pltpu.VMEM)
SIDE = 4
OWN = 8
T = 128
TB = 32
LIMIT = 60 * 1024 * 1024
DIRS = (0, 1)


def step(d):
    return 1 if d == 0 else SIDE - 1


class Copies:
    def __init__(self, send, recv):
        self.send, self.recv, self.used, self.open = send, recv, 0, []

    def slot(self):
        self.used += 1
        return self.used - 1

    def start(self, slot, src, dst, to):
        copy = pltpu.make_async_remote_copy(
            src_ref=src,
            dst_ref=dst,
            send_sem=self.send.at[slot],
            recv_sem=self.recv.at[slot],
            device_id=to,
            device_id_type=MESH,
        )
        copy.start()
        self.open.append(copy)
        return copy

    def finish(self):
        for copy in self.open:
            copy.wait_send()


def greet(peers):
    barrier = pltpu.get_barrier_semaphore()
    for peer in peers:
        pl.semaphore_signal(barrier, inc=1, device_id=peer, device_id_type=MESH)
    pl.semaphore_wait(barrier, len(peers))


def gather_kernel(v_ref, out, send, recv):
    me = lax.axis_index("row")
    z, core = me // 2, lax.rem(me, 2)
    other = 1 - core

    def at(d):
        return lax.rem(z + step(d), SIDE)

    near = [{"row": at(d) * 2 + core} for d in DIRS]
    mate = {"row": z * 2 + other}
    opp = lax.rem(z + 2, SIDE)
    out[me] = v_ref[...].astype(BF16)
    greet(near + [mate])
    copies = Copies(send, recv)

    def push(slot, index, part, to):
        ref = out.at[index, part]
        return copies.start(slot, ref, ref, to)

    full = pl.ds(0, OWN)
    part = [pl.ds(0, OWN // 2), pl.ds(OWN // 2, OWN // 2)]
    hop = [push(copies.slot(), me, full, near[d]) for d in DIRS]
    mates = [push(copies.slot(), me, full, mate)]
    far = []
    for d in DIRS:
        index = at(1 - d) * 2 + core
        hop[d].wait_recv()
        far.append(push(copies.slot(), index, part[d], near[d]))
        mates.append(push(copies.slot(), index, full, mate))
    for d in DIRS:
        far[d].wait_recv()
        mates.append(push(copies.slot(), opp * 2 + core, part[d], mate))
    for copy in mates:
        copy.wait_recv()
    copies.finish()


def gather(v):
    count = 2 + 1 + 2 + 2 + 2
    return pl.pallas_call(
        gather_kernel,
        in_specs=[VM],
        out_specs=VM,
        out_shape=jax.ShapeDtypeStruct((2 * SIDE, OWN, T, T), BF16),
        scratch_shapes=[pltpu.SemaphoreType.DMA((count,)), pltpu.SemaphoreType.DMA((count,))],
        compiler_params=pltpu.CompilerParams(
            collective_id=0, has_side_effects=True, vmem_limit_bytes=LIMIT
        ),
        name="gather_video",
    )(v)


def forward_kernel(
    count, rows, cols, tiles, panel, out, row_mass, col_mass, total, row_sum, col_sum
):
    g = pl.program_id(0)
    n = count[0]
    n_rows, n_cols = out.shape[0], col_mass.shape[0]

    @pl.when(g == 0)
    def _():
        total[...] = jnp.zeros_like(total)
        row_sum[...] = jnp.zeros_like(row_sum)
        col_sum[...] = jnp.zeros_like(col_sum)

    @pl.when(g * TB < n)
    def _():
        sums = lax.dot_general(
            jnp.ones((8, T), BF16),
            tiles[...].reshape(TB * T, T),
            (((1,), (1,)), ((), ())),
            preferred_element_type=F32,
        )
        todo = []
        for s in range(TB):
            live = g * TB + s < n
            col = cols[g * TB + s]
            prod = jnp.dot(tiles[s], panel[col], preferred_element_type=F32)
            down = jnp.sum(tiles[s].astype(F32).reshape(T // 8, 8, T), axis=0)
            row = jnp.where(live, rows[g * TB + s], n_rows)
            todo.append((row, jnp.where(live, col, n_cols), prod, down))
        for s, (row, col, prod, down) in enumerate(todo):
            total[row] += prod
            row_sum[row] += sums[:, s * T : (s + 1) * T]
            col_sum[col] += down

    @pl.when(g == pl.num_programs(0) - 1)
    def _():
        @pl.loop(0, n_rows // 8)
        def _(i):
            out[pl.ds(i * 8, 8)] = total[pl.ds(i * 8, 8)].astype(BF16)

        row_mass[...] = jnp.sum(row_sum[:n_rows], axis=1) * 0.125
        col_mass[...] = jnp.sum(col_sum[:n_cols], axis=1)


def forward(count, rows, cols, tiles, panel, n_rows, n_cols):
    slots = tiles.shape[0]
    return pl.pallas_call(
        forward_kernel,
        grid_spec=pltpu.PrefetchScalarGridSpec(
            num_scalar_prefetch=3,
            grid=(slots // TB,),
            in_specs=[pl.BlockSpec((TB, T, T), lambda g, *_: (g, 0, 0)), VM],
            out_specs=[VM, VM, VM],
            scratch_shapes=[
                pltpu.VMEM((n_rows + 1, T, T), F32),
                pltpu.VMEM((n_rows + 1, 8, T), F32),
                pltpu.VMEM((n_cols + 1, 8, T), F32),
            ],
        ),
        out_shape=[
            jax.ShapeDtypeStruct((n_rows, T, T), BF16),
            jax.ShapeDtypeStruct((n_rows, T), F32),
            jax.ShapeDtypeStruct((n_cols, T), F32),
        ],
        compiler_params=pltpu.CompilerParams(vmem_limit_bytes=LIMIT),
        name="forward_tiles",
    )(count, rows, cols, tiles, panel)


def backward_kernel(count, rows, cols, tiles, panel, out, total):
    g = pl.program_id(0)
    n = count[0]
    n_cols = out.shape[0]

    @pl.when(g == 0)
    def _():
        total[...] = jnp.zeros_like(total)

    @pl.when(g * TB < n)
    def _():
        todo = []
        for s in range(TB):
            prod = jnp.dot(panel[rows[g * TB + s]], tiles[s], preferred_element_type=F32)
            todo.append((jnp.where(g * TB + s < n, cols[g * TB + s], n_cols), prod))
        for col, prod in todo:
            total[col] += prod

    @pl.when(g == pl.num_programs(0) - 1)
    def _():
        @pl.loop(0, n_cols // 8)
        def _(i):
            out[pl.ds(i * 8, 8)] = total[pl.ds(i * 8, 8)].astype(BF16)


def backward(count, rows, cols, tiles, panel, n_cols):
    slots = tiles.shape[0]
    return pl.pallas_call(
        backward_kernel,
        grid_spec=pltpu.PrefetchScalarGridSpec(
            num_scalar_prefetch=3,
            grid=(slots // TB,),
            in_specs=[pl.BlockSpec((TB, T, T), lambda g, *_: (g, 0, 0)), VM],
            out_specs=VM,
            scratch_shapes=[pltpu.VMEM((n_cols + 1, T, T), F32)],
        ),
        out_shape=jax.ShapeDtypeStruct((n_cols, T, T), BF16),
        compiler_params=pltpu.CompilerParams(vmem_limit_bytes=LIMIT),
        name="backward_tiles",
    )(count, rows, cols, tiles, panel)


def blend(total, mass, seeds):
    labels = (lax.broadcasted_iota(jnp.int32, total.shape, 0) == seeds).astype(F32)
    return total * (0.75 / jnp.sqrt(mass)) + 0.25 * labels


QUART = OWN // 4


def exchange_kernel(part, mass_in, seeds, full, own, *scratch):
    (
        opp1, plain1, merged1, edge1, sum1, half1, opp2, plain2, merged2, edge2, tot,
        mass_far, mass_edge, mass_sum, mass_hop, mass_far2, mass_edge2, mass_hop2, send, recv,
    ) = scratch
    me = lax.axis_index("col")
    pos = {"y": me // SIDE, "x": lax.rem(me, SIDE)}

    def at(axis, k):
        return lax.rem(pos[axis] + k, SIDE)

    def peer(axis, d):
        y, x = pos["y"], pos["x"]
        if axis == "y":
            y = at("y", step(d))
        else:
            x = at("x", step(d))
        return {"col": y * SIDE + x}

    greet([peer(axis, d) for axis in "xy" for d in DIRS])
    copies = Copies(send, recv)
    halves = (("x", "y"), ("y", "x"))

    def tiles_of(h, d):
        return pl.ds((2 * h + d) * QUART, QUART)

    def unit(h, index, d):
        return part.at[:, index, tiles_of(h, d)] if h == 0 else part.at[index, :, tiles_of(h, d)]

    y, x = pos["y"], pos["x"]
    c_far = copies.start(copies.slot(), mass_in.at[:, at("x", 2)], mass_far, peer("x", 0))
    c_hop = copies.start(copies.slot(), mass_in.at[:, at("x", 3)], mass_hop.at[1], peer("x", 1))

    c_opp, c_plain, c_merged = {}, {}, {}
    both = [(h, d) for d in DIRS for h in (0, 1)]
    for h, d in both:
        axis = halves[h][0]
        to = peer(axis, d)
        c_opp[h, d] = copies.start(
            copies.slot(), unit(h, at(axis, 2), d), opp1.at[h, d], to
        )
    for h, d in both:
        axis = halves[h][0]
        c_plain[h, d] = copies.start(
            copies.slot(), unit(h, at(axis, step(d)), 1 - d), plain1.at[h, d], peer(axis, d)
        )

    c_far.wait_recv()
    mass_edge[...] = mass_far[...] + mass_in[:, at("x", 1)]
    c_merge = copies.start(copies.slot(), mass_edge, mass_hop.at[0], peer("x", 0))

    for h, d in both:
        axis = halves[h][0]
        index = at(axis, step(d))
        c_opp[h, d].wait_recv()
        mine = unit(h, index, d)

        @pl.loop(0, SIDE)
        def _(k):
            edge1[h, d, k] = (mine[k].astype(F32) + opp1[h, d, k].astype(F32)).astype(BF16)

        c_merged[h, d] = copies.start(
            copies.slot(), edge1.at[h, d], merged1.at[h, d], peer(axis, d)
        )

    c_hop.wait_recv()
    c_merge.wait_recv()
    mass_sum[...] = mass_in[:, x] + mass_hop[0] + mass_hop[1]
    c_far = copies.start(copies.slot(), mass_sum.at[at("y", 2)], mass_far2, peer("y", 0))
    c_hop = copies.start(copies.slot(), mass_sum.at[at("y", 3)], mass_hop2.at[1], peer("y", 1))

    for h, d in both:
        c_plain[h, 1 - d].wait_recv()
        c_merged[h, d].wait_recv()
        mine = unit(h, pos[halves[h][0]], d)

        @pl.loop(0, SIDE)
        def _(k):
            value = (
                mine[k].astype(F32)
                + merged1[h, d, k].astype(F32)
                + plain1[h, 1 - d, k].astype(F32)
            )
            sum1[h, d, k] = value
            half1[h, d, k] = value.astype(BF16)

        axis = halves[h][1]
        c_opp[h, d] = copies.start(
            copies.slot(), half1.at[h, d, at(axis, 2)], opp2.at[h, d], peer(axis, d)
        )
        c_plain[h, 1 - d] = copies.start(
            copies.slot(),
            half1.at[h, d, at(axis, step(1 - d))],
            plain2.at[h, 1 - d],
            peer(axis, 1 - d),
        )

    c_far.wait_recv()
    mass_edge2[...] = mass_far2[...] + mass_sum[at("y", 1)]
    c_merge = copies.start(copies.slot(), mass_edge2, mass_hop2.at[0], peer("y", 0))

    for h, d in both:
        axis = halves[h][1]
        c_opp[h, d].wait_recv()
        edge2[h, d] = (sum1[h, d, at(axis, step(d))] + opp2[h, d].astype(F32)).astype(BF16)
        c_merged[h, d] = copies.start(
            copies.slot(), edge2.at[h, d], merged2.at[h, d], peer(axis, d)
        )

    c_hop.wait_recv()
    c_merge.wait_recv()
    mass = mass_sum[y] + mass_hop2[0] + mass_hop2[1]

    for h, d in both:
        axis = halves[h][1]
        c_plain[h, 1 - d].wait_recv()
        c_merged[h, d].wait_recv()
        tot[h, d] = (
            sum1[h, d, pos[axis]] + merged2[h, d].astype(F32) + plain2[h, 1 - d].astype(F32)
        )
        for i in range(QUART):
            t = (2 * h + d) * QUART + i
            scores = blend(tot[h, d, i].T, mass[t : t + 1], seeds[t : t + 1])
            own[t] = scores
            full[y, x, t] = scores.astype(BF16)

    def place(h, k, u, ds):
        return full.at[k, u, ds] if h == 0 else full.at[u, k, ds]

    def push(h, k, u, ds, axis, d):
        ref = place(h, k, u, ds)
        return copies.start(copies.slot(), ref, ref, peer(axis, d))

    half = [pl.ds(0, 2 * QUART), pl.ds(2 * QUART, 2 * QUART)]
    c_a, c_af, c_b, c_bf = {}, {}, {}, {}
    for h in (0, 1):
        second, first = halves[h]
        for d in DIRS:
            c_a[h, d] = push(h, pos[first], pos[second], half[h], first, d)
    for h in (0, 1):
        second, first = halves[h]
        for d in DIRS:
            c_b[h, "own", d] = push(h, pos[first], pos[second], half[h], second, d)
    for h, d in both:
        second, first = halves[h]
        c_a[h, d].wait_recv()
        k = at(first, step(1 - d))
        c_af[h, d] = push(h, k, pos[second], tiles_of(h, d), first, d)
        for e in DIRS:
            c_b[h, d, e] = push(h, k, pos[second], half[h], second, e)
    for h, d in both:
        second, first = halves[h]
        c_b[h, "own", d].wait_recv()
        c_bf[h, "own", d] = push(
            h, pos[first], at(second, step(1 - d)), tiles_of(h, d), second, d
        )
    for h, d in both:
        second, first = halves[h]
        c_af[h, d].wait_recv()
        for e in DIRS:
            c_b[h, "far", d, e] = push(
                h, at(first, 2), pos[second], tiles_of(h, d), second, e
            )
    for h, e in both:
        second, first = halves[h]
        for d in DIRS:
            c_b[h, d, e].wait_recv()
            c_bf[h, d, e] = push(
                h, at(first, step(1 - d)), at(second, step(1 - e)), tiles_of(h, e), second, e
            )
    for h, e in both:
        second, first = halves[h]
        c_b[h, "far", e, e].wait_recv()
        c_bf[h, "far", e] = push(
            h, at(first, 2), at(second, step(1 - e)), tiles_of(h, e), second, e
        )
    for h, d in both:
        c_b[h, "far", d, 1 - d].wait_recv()
    for copy in c_bf.values():
        copy.wait_recv()
    copies.finish()


def exchange(part, mass, seeds):
    count = 6 + 4 * 6 + 2 * (2 + 2 + 2 + 4 + 2 + 4 + 4 + 2)
    unit = (2, 2, SIDE, QUART, T, T)
    small = (2, 2, QUART, T, T)
    return pl.pallas_call(
        exchange_kernel,
        in_specs=[VM, VM, VM],
        out_specs=[VM, VM],
        out_shape=[
            jax.ShapeDtypeStruct((SIDE, SIDE, OWN, T, T), BF16),
            jax.ShapeDtypeStruct((OWN, T, T), F32),
        ],
        scratch_shapes=[
            pltpu.VMEM(unit, BF16),
            pltpu.VMEM(unit, BF16),
            pltpu.VMEM(unit, BF16),
            pltpu.VMEM(unit, BF16),
            pltpu.VMEM(unit, F32),
            pltpu.VMEM(unit, BF16),
            pltpu.VMEM(small, BF16),
            pltpu.VMEM(small, BF16),
            pltpu.VMEM(small, BF16),
            pltpu.VMEM(small, BF16),
            pltpu.VMEM(small, F32),
            pltpu.VMEM((SIDE, OWN, T), F32),
            pltpu.VMEM((SIDE, OWN, T), F32),
            pltpu.VMEM((SIDE, OWN, T), F32),
            pltpu.VMEM((2, SIDE, OWN, T), F32),
            pltpu.VMEM((OWN, T), F32),
            pltpu.VMEM((OWN, T), F32),
            pltpu.VMEM((2, OWN, T), F32),
            pltpu.SemaphoreType.DMA((count,)),
            pltpu.SemaphoreType.DMA((count,)),
        ],
        compiler_params=pltpu.CompilerParams(
            collective_id=1, has_side_effects=True, vmem_limit_bytes=LIMIT
        ),
        name="exchange_audio",
    )(part, mass, seeds)


def reduce_kernel(part, mass_in, seeds, out, *scratch):
    (
        swap, total, half, opp, plain, merged, edge,
        mass_swap, mass_tot, mass_far, mass_edge, mass_hop, send, recv,
    ) = scratch
    me = lax.axis_index("row")
    z, core = me // 2, lax.rem(me, 2)
    other = 1 - core

    def at(k):
        return lax.rem(z + k, SIDE)

    near = [{"row": at(step(d)) * 2 + core} for d in DIRS]
    mate = {"row": z * 2 + other}
    greet(near + [mate])
    copies = Copies(send, recv)
    piece = [pl.ds(0, OWN // 2), pl.ds(OWN // 2, OWN // 2)]

    c_mass = copies.start(copies.slot(), mass_in.at[:, other], mass_swap, mate)
    c_swap = []
    for i, k in enumerate((2, 1, 3, 0)):
        c_swap.append(
            copies.start(copies.slot(), part.at[at(k), other], swap.at[i], mate)
        )

    def add_mate(i, k):
        c_swap[i].wait_recv()
        index = at(k)

        @pl.loop(0, OWN)
        def _(t):
            value = part[index, core, t].astype(F32) + swap[i, t].astype(F32)
            total[i, t] = value
            half[i, t] = value.astype(BF16)

    add_mate(0, 2)
    c_opp = [copies.start(copies.slot(), half.at[0, piece[d]], opp.at[d], near[d]) for d in DIRS]
    c_plain = []
    for d in DIRS:
        add_mate(1 + d, step(d))
        c_plain.append(
            copies.start(copies.slot(), half.at[1 + d, piece[1 - d]], plain.at[d], near[d])
        )
    c_mass.wait_recv()
    mass_tot[...] = mass_in[:, core] + mass_swap[...]
    c_far = copies.start(copies.slot(), mass_tot.at[at(2)], mass_far, near[0])
    c_hop = copies.start(copies.slot(), mass_tot.at[at(3)], mass_hop.at[1], near[1])
    add_mate(3, 0)
    c_merged = []
    for d in DIRS:
        c_opp[d].wait_recv()

        @pl.loop(0, OWN // 2)
        def _(t):
            edge[d, t] = (total[1 + d, d * (OWN // 2) + t] + opp[d, t].astype(F32)).astype(BF16)

        c_merged.append(copies.start(copies.slot(), edge.at[d], merged.at[d], near[d]))
    c_far.wait_recv()
    mass_edge[...] = mass_far[...] + mass_tot[at(1)]
    c_merge = copies.start(copies.slot(), mass_edge, mass_hop.at[0], near[0])
    c_hop.wait_recv()
    c_merge.wait_recv()
    mass = mass_tot[z] + mass_hop[0] + mass_hop[1]
    for d in DIRS:
        c_plain[1 - d].wait_recv()
        c_merged[d].wait_recv()
        for i in range(OWN // 2):
            t = d * (OWN // 2) + i
            value = total[3, t] + merged[d, i].astype(F32) + plain[1 - d, i].astype(F32)
            out[t] = blend(value, mass[t : t + 1], seeds[t : t + 1]).T
    copies.finish()


def reduce(part, mass, seeds):
    count = 1 + 4 + 2 + 2 + 2 + 2 + 1
    unit = (SIDE, OWN, T, T)
    small = (2, OWN // 2, T, T)
    return pl.pallas_call(
        reduce_kernel,
        in_specs=[VM, VM, VM],
        out_specs=VM,
        out_shape=jax.ShapeDtypeStruct((OWN, T, T), F32),
        scratch_shapes=[
            pltpu.VMEM(unit, BF16),
            pltpu.VMEM(unit, F32),
            pltpu.VMEM(unit, BF16),
            pltpu.VMEM(small, BF16),
            pltpu.VMEM(small, BF16),
            pltpu.VMEM(small, BF16),
            pltpu.VMEM(small, BF16),
            pltpu.VMEM((SIDE, OWN, T), F32),
            pltpu.VMEM((SIDE, OWN, T), F32),
            pltpu.VMEM((OWN, T), F32),
            pltpu.VMEM((OWN, T), F32),
            pltpu.VMEM((2, OWN, T), F32),
            pltpu.SemaphoreType.DMA((count,)),
            pltpu.SemaphoreType.DMA((count,)),
        ],
        compiler_params=pltpu.CompilerParams(
            collective_id=2, has_side_effects=True, vmem_limit_bytes=LIMIT
        ),
        name="reduce_video",
    )(part, mass, seeds)


def turn_kernel(x, out):
    for t in range(OWN):
        out[t] = x[t].T


def turn(x):
    return pl.pallas_call(
        turn_kernel,
        in_specs=[VM],
        out_specs=VM,
        out_shape=jax.ShapeDtypeStruct(x.shape, F32),
        name="turn",
    )(x)


def body(video_scores_in, audio_seed, video_seed, tile_values, tile_rows, tile_cols, tile_count):
    tiles, rows, cols = tile_values[0, 0], tile_rows[0, 0], tile_cols[0, 0]
    count = tile_count[0]
    n_rows, n_cols = SIDE * SIDE * OWN, 2 * SIDE * OWN
    panel = gather(video_scores_in.reshape(OWN, T, T)).reshape(n_cols, T, T)
    part, row_mass, col_mass = forward(count, rows, cols, tiles, panel, n_rows, n_cols)
    full, own = exchange(
        part.reshape(SIDE, SIDE, OWN, T, T),
        row_mass.reshape(SIDE, SIDE, OWN, T),
        audio_seed.reshape(OWN, T),
    )
    audio_scores = turn(own).reshape(OWN * T, T)
    back = backward(count, rows, cols, tiles, full.reshape(n_rows, T, T), n_cols)
    video_scores = reduce(
        back.reshape(SIDE, 2, OWN, T, T),
        col_mass.reshape(SIDE, 2, OWN, T),
        video_seed.reshape(OWN, T),
    ).reshape(OWN * T, T)
    return (audio_scores, video_scores)


def solution(mesh):
    in_specs = (
        P(("col", "row"), None),
        P(("row", "col")),
        P(("col", "row")),
        P("row", "col", None, None, None),
        P("row", "col", None),
        P("row", "col", None),
        P("row", "col"),
    )
    out_specs = (P(("row", "col"), None), P(("col", "row"), None))
    return jax.shard_map(body, mesh=mesh, in_specs=in_specs, out_specs=out_specs, check_vma=False)
```

```python
import functools

import jax
import jax.numpy as jnp
from jax import lax
from jax.experimental import pallas as pl
from jax.experimental.pallas import tpu as pltpu
from jax.sharding import PartitionSpec as P

MESH = pl.DeviceIdType.MESH
F32, BF16 = jnp.float32, jnp.bfloat16
VM = pl.BlockSpec(memory_space=pltpu.VMEM)
SM = pl.BlockSpec(memory_space=pltpu.SMEM)
SIDE = 4
OWN = 8
QUART = OWN // 4
T = 128
CHUNK = 32
UNROLL = 16
LIMIT = 67043328
DIRS = (0, 1)


def step(d):
    return 1 if d == 0 else SIDE - 1


class Copies:
    def __init__(self, send, recv):
        self.send, self.recv, self.used, self.open = send, recv, 0, []

    def slot(self):
        self.used += 1
        return self.used - 1

    def start(self, slot, src, dst, to):
        copy = pltpu.make_async_remote_copy(
            src_ref=src,
            dst_ref=dst,
            send_sem=self.send.at[slot],
            recv_sem=self.recv.at[slot],
            device_id=to,
            device_id_type=MESH,
        )
        copy.start()
        self.open.append(copy)
        return copy

    def finish(self):
        for copy in self.open:
            copy.wait_send()


def greet(peers):
    barrier = pltpu.get_barrier_semaphore()
    for peer in peers:
        pl.semaphore_signal(barrier, inc=1, device_id=peer, device_id_type=MESH)
    pl.semaphore_wait(barrier, len(peers))


def plan_kernel(count, rows, cols, by_row, by_col, in_row, in_col):
    slots = rows.shape[1]
    wide = by_row.shape[1]
    lane = lax.broadcasted_iota(jnp.int32, (1, slots), 1)
    live = lane < count[0, 0]
    before = (
        lax.broadcasted_iota(jnp.int32, (slots, slots), 0)
        < lax.broadcasted_iota(jnp.int32, (slots, slots), 1)
    ).astype(BF16)
    below = (
        lax.broadcasted_iota(jnp.int32, (T, T), 0) > lax.broadcasted_iota(jnp.int32, (T, T), 1)
    ).astype(F32)

    def one(key, other, member, index):
        key = jnp.where(live, key, 1023)
        hit = (lax.broadcasted_iota(jnp.int32, (T, slots), 0) == key).astype(F32)
        member[...] = hit[: member.shape[0]].astype(BF16)
        rank = jnp.dot(hit.astype(BF16), before, preferred_element_type=F32)
        rank = jnp.sum(hit * rank, axis=0, keepdims=True)
        size = jnp.sum(hit, axis=1, keepdims=True)
        pairs = jnp.broadcast_to(jnp.floor((size + 1.0) * 0.5), (T, T))
        base = jnp.dot(
            below, pairs, preferred_element_type=F32, precision=lax.Precision.HIGHEST
        )
        start = jnp.sum(hit * base[:, :1], axis=0, keepdims=True)
        place = jnp.where(live, 2.0 * start + rank, -1.0)
        place = jnp.broadcast_to(place, (T, slots)).T
        high = lane // T
        part = lax.broadcasted_iota(jnp.int32, (8, slots), 0)
        facts = jnp.where(part == 0, high, lane - high * T)
        facts = jnp.where(part == 2, other, facts)
        facts = jnp.where(part == 3, 1, facts)
        facts = jnp.where(part == 4, (rank == 0.0).astype(jnp.int32), facts)
        facts = facts.astype(F32).astype(BF16)
        last = (base + pairs - 1.0).T
        row = lax.broadcasted_iota(jnp.int32, (8, T), 0)
        for c in range(wide // T):
            spot = lax.broadcasted_iota(jnp.int32, (slots, T), 1) + c * T
            chosen = (place == spot.astype(F32)).astype(BF16)
            got = jnp.dot(facts, chosen, preferred_element_type=F32)
            tile = got[0:1] * T + got[1:2] + slots * (1.0 - got[3:4])
            value = jnp.where(row == 0, tile, got[2:3])
            value = jnp.where(row == 2, 1.0 - got[4:5], value)
            value = jnp.where(row == 3, last[:8], value)
            index[:, c * T : (c + 1) * T] = value.astype(jnp.int32)

    one(rows[...], cols[...], in_row, by_row)
    one(cols[...], rows[...], in_col, by_col)


def plan(count, rows, cols, n_rows, n_cols):
    slots = rows.shape[1]
    wide = slots + n_rows
    return pl.pallas_call(
        plan_kernel,
        in_specs=[SM, VM, VM],
        out_specs=[VM] * 4,
        out_shape=[
            jax.ShapeDtypeStruct((8, wide), jnp.int32),
            jax.ShapeDtypeStruct((8, wide), jnp.int32),
            jax.ShapeDtypeStruct((n_rows, slots), BF16),
            jax.ShapeDtypeStruct((n_cols, slots), BF16),
        ],
        compiler_params=pltpu.CompilerParams(vmem_limit_bytes=16 * 1024 * 1024),
        name="plan",
    )(count, rows, cols)


def blend(total, mass, seeds):
    labels = (lax.broadcasted_iota(jnp.int32, total.shape, 0) == seeds).astype(F32)
    return total * (0.75 / jnp.sqrt(mass)) + 0.25 * labels


def sweep_kernel(
    by_row, by_col, v_in, tiles_in, in_row, in_col, audio_seeds, video_seeds,
    audio_out, video_out,
    tiles, held, panel, part, full, back, acc, row_sums, col_sums, mass_in, mass_col,
    opp1, plain1, merged1, edge1, sum1, half1, opp2, plain2, merged2, edge2,
    mass_far, mass_edge, mass_sum, mass_hop, mass_far2, mass_edge2, mass_hop2,
    swap, total, half, opp, plain, merged, edge,
    r_swap, r_tot, r_far, r_edge, r_hop,
    send, recv, load,
):
    slots = tiles_in.shape[0]
    n_chunks = slots // CHUNK
    n_cols = panel.shape[0]
    row_id, col_id = lax.axis_index("row"), lax.axis_index("col")
    core = lax.rem(row_id, 2)
    pos = {"y": col_id // SIDE, "x": lax.rem(col_id, SIDE), "z": row_id // 2}
    y, x, z = pos["y"], pos["x"], pos["z"]

    def at(axis, k):
        return lax.rem(pos[axis] + k, SIDE)

    def peer(axis, d):
        if axis == "y":
            return {"col": at("y", step(d)) * SIDE + x}
        if axis == "x":
            return {"col": y * SIDE + at("x", step(d))}
        return {"row": at("z", step(d)) * 2 + core}

    mate = {"row": z * 2 + 1 - core}
    copies = Copies(send, recv)

    def start(src, dst, to):
        return copies.start(copies.slot(), src, dst, to)

    loads = []
    for i in range(n_chunks):
        span = pl.ds(i * CHUNK, CHUNK)
        copy = pltpu.make_async_copy(tiles_in.at[span], tiles.at[span], load.at[i])
        copy.start()
        loads.append(copy)
    tiles[slots] = jnp.zeros((T, T), BF16)

    panel[pl.ds(row_id * OWN, OWN)] = v_in[...].astype(BF16)
    greet([peer(axis, d) for axis in "xyz" for d in DIRS] + [mate])

    def push_video(index, first, size, to):
        ref = panel.at[pl.ds(index * OWN + first, size)]
        return start(ref, ref, to)

    def tile_sums(chunks):
        for i in chunks:
            loads[i].wait()

        @pl.loop(chunks[0], chunks[-1] + 1)
        def _(i):
            sums = lax.dot_general(
                jnp.ones((8, T), BF16),
                tiles[pl.ds(i * CHUNK, CHUNK)].reshape(CHUNK * T, T),
                (((1,), (1,)), ((), ())),
                preferred_element_type=F32,
            )
            for s in range(CHUNK):
                row_sums[pl.ds(i * CHUNK + s, 1)] = sums[0:1, s * T : (s + 1) * T]
                col_sums[pl.ds(i * CHUNK + s, 1)] = jnp.sum(
                    tiles[i * CHUNK + s].astype(F32), axis=0, keepdims=True
                )

    cut = (n_chunks * 9 // 20, n_chunks * 15 // 20)
    hop = [push_video(row_id, 0, OWN, peer("z", d)) for d in DIRS]
    mates = [push_video(row_id, 0, OWN, mate)]
    tile_sums(range(0, cut[0]))
    far = []
    for d in DIRS:
        index = at("z", step(1 - d)) * 2 + core
        hop[d].wait_recv()
        far.append(push_video(index, d * OWN // 2, OWN // 2, peer("z", d)))
        mates.append(push_video(index, 0, OWN, mate))
    tile_sums(range(cut[0], cut[1]))
    for d in DIRS:
        far[d].wait_recv()
        mates.append(push_video(at("z", 2) * 2 + core, d * OWN // 2, OWN // 2, mate))
    tile_sums(range(cut[1], n_chunks))

    def gathered(member, sums):
        value = sums[pl.ds(0, slots)]
        upper = value.astype(BF16)
        lower = (value - upper.astype(F32)).astype(BF16)
        return jnp.dot(member[...], upper, preferred_element_type=F32) + jnp.dot(
            member[...], lower, preferred_element_type=F32
        )

    mass_in[...] = gathered(in_row, row_sums).reshape(mass_in.shape)
    mass_col[...] = gathered(in_col, col_sums).reshape(mass_col.shape)

    c_far = start(mass_in.at[:, at("x", 2)], mass_far, peer("x", 0))
    c_hop = start(mass_in.at[:, at("x", 3)], mass_hop.at[1], peer("x", 1))
    r_mate = start(mass_col.at[:, 1 - core], r_swap, mate)
    for copy in mates:
        copy.wait_recv()

    def products(index, count, left, right):
        acc[...] = jnp.zeros_like(acc)

        @pl.loop(0, count // UNROLL)
        def _(i):
            prods = []
            for u in range(UNROLL):
                g = (i * UNROLL + u) * 2
                a, b = (index[0, g], index[1, g]), (index[0, g + 1], index[1, g + 1])
                prods.append(
                    jnp.dot(
                        jnp.concatenate([left(*a), left(*b)], axis=1),
                        jnp.concatenate([right(*a), right(*b)], axis=0),
                        preferred_element_type=F32,
                    )
                )
            value = acc[...]
            for u in range(UNROLL):
                g = i * UNROLL + u
                value = value * index[2, g * 2].astype(F32) + prods[u]
                held[g] = value.astype(BF16)
            acc[...] = value

    products(by_row, held.shape[0], lambda t, c: tiles[t], lambda t, c: panel[c])

    @pl.loop(0, SIDE * SIDE)
    def _(o):
        for j in range(OWN):
            part[o // SIDE, lax.rem(o, SIDE), j] = held[by_row[3, o * OWN + j]]

    halves = (("x", "y"), ("y", "x"))

    def tiles_of(h, d):
        return pl.ds((2 * h + d) * QUART, QUART)

    def unit(h, index, d):
        return part.at[:, index, tiles_of(h, d)] if h == 0 else part.at[index, :, tiles_of(h, d)]

    c_opp, c_plain, c_merged = {}, {}, {}
    both = [(h, d) for d in DIRS for h in (0, 1)]
    for h, d in both:
        axis = halves[h][0]
        c_opp[h, d] = start(unit(h, at(axis, 2), d), opp1.at[h, d], peer(axis, d))
    for h, d in both:
        axis = halves[h][0]
        c_plain[h, d] = start(
            unit(h, at(axis, step(d)), 1 - d), plain1.at[h, d], peer(axis, d)
        )

    c_far.wait_recv()
    mass_edge[...] = mass_far[...] + mass_in[:, at("x", 1)]
    c_merge = start(mass_edge, mass_hop.at[0], peer("x", 0))
    r_mate.wait_recv()
    r_tot[...] = mass_col[:, core] + r_swap[...]
    r_c_far = start(r_tot.at[at("z", 2)], r_far, peer("z", 0))
    r_c_hop = start(r_tot.at[at("z", 3)], r_hop.at[1], peer("z", 1))

    for h, d in both:
        axis = halves[h][0]
        index = at(axis, step(d))
        c_opp[h, d].wait_recv()
        mine = unit(h, index, d)

        @pl.loop(0, SIDE)
        def _(k):
            edge1[h, d, k] = (mine[k].astype(F32) + opp1[h, d, k].astype(F32)).astype(BF16)

        c_merged[h, d] = start(edge1.at[h, d], merged1.at[h, d], peer(axis, d))

    c_hop.wait_recv()
    c_merge.wait_recv()
    mass_sum[...] = mass_in[:, x] + mass_hop[0] + mass_hop[1]
    c_far = start(mass_sum.at[at("y", 2)], mass_far2, peer("y", 0))
    c_hop = start(mass_sum.at[at("y", 3)], mass_hop2.at[1], peer("y", 1))
    r_c_far.wait_recv()
    r_edge[...] = r_far[...] + r_tot[at("z", 1)]
    r_c_merge = start(r_edge, r_hop.at[0], peer("z", 0))

    for h, d in both:
        c_plain[h, 1 - d].wait_recv()
        c_merged[h, d].wait_recv()
        mine = unit(h, pos[halves[h][0]], d)

        @pl.loop(0, SIDE)
        def _(k):
            value = (
                mine[k].astype(F32)
                + merged1[h, d, k].astype(F32)
                + plain1[h, 1 - d, k].astype(F32)
            )
            sum1[h, d, k] = value
            half1[h, d, k] = value.astype(BF16)

        axis = halves[h][1]
        c_opp[h, d] = start(half1.at[h, d, at(axis, 2)], opp2.at[h, d], peer(axis, d))
        c_plain[h, 1 - d] = start(
            half1.at[h, d, at(axis, step(1 - d))], plain2.at[h, 1 - d], peer(axis, 1 - d)
        )

    c_far.wait_recv()
    mass_edge2[...] = mass_far2[...] + mass_sum[at("y", 1)]
    c_merge = start(mass_edge2, mass_hop2.at[0], peer("y", 0))

    for h, d in both:
        axis = halves[h][1]
        c_opp[h, d].wait_recv()
        edge2[h, d] = (sum1[h, d, at(axis, step(d))] + opp2[h, d].astype(F32)).astype(BF16)
        c_merged[h, d] = start(edge2.at[h, d], merged2.at[h, d], peer(axis, d))

    c_hop.wait_recv()
    c_merge.wait_recv()
    mass = mass_sum[y] + mass_hop2[0] + mass_hop2[1]
    r_c_hop.wait_recv()
    r_c_merge.wait_recv()
    mass_video = r_tot[z] + r_hop[0] + r_hop[1]

    def spot(h, k, u):
        return (k * SIDE + u) * OWN if h == 0 else (u * SIDE + k) * OWN

    for h, d in both:
        axis = halves[h][1]
        c_plain[h, 1 - d].wait_recv()
        c_merged[h, d].wait_recv()
        for i in range(QUART):
            t = (2 * h + d) * QUART + i
            value = (
                sum1[h, d, pos[axis], i]
                + merged2[h, d, i].astype(F32)
                + plain2[h, 1 - d, i].astype(F32)
            )
            scores = blend(value.T, mass[t : t + 1], audio_seeds[t : t + 1])
            audio_out[t] = scores
            full[col_id * OWN + t] = scores.astype(BF16)

    def push(h, k, u, d, axis, way):
        if d is None:
            span = pl.ds(spot(h, k, u) + 2 * h * QUART, 2 * QUART)
        else:
            span = pl.ds(spot(h, k, u) + (2 * h + d) * QUART, QUART)
        ref = full.at[span]
        return start(ref, ref, peer(axis, way))

    c_a, c_af, c_b, c_bf = {}, {}, {}, {}
    for h in (0, 1):
        second, first = halves[h]
        for d in DIRS:
            c_a[h, d] = push(h, pos[first], pos[second], None, first, d)
    for h in (0, 1):
        second, first = halves[h]
        for d in DIRS:
            c_b[h, "own", d] = push(h, pos[first], pos[second], None, second, d)
    for h, d in both:
        second, first = halves[h]
        c_a[h, d].wait_recv()
        k = at(first, step(1 - d))
        c_af[h, d] = push(h, k, pos[second], d, first, d)
        for e in DIRS:
            c_b[h, d, e] = push(h, k, pos[second], None, second, e)
    for h, d in both:
        second, first = halves[h]
        c_b[h, "own", d].wait_recv()
        c_bf[h, "own", d] = push(h, pos[first], at(second, step(1 - d)), d, second, d)
    for h, d in both:
        second, first = halves[h]
        c_af[h, d].wait_recv()
        for e in DIRS:
            c_b[h, "far", d, e] = push(h, at(first, 2), pos[second], d, second, e)
    for h, e in both:
        second, first = halves[h]
        for d in DIRS:
            c_b[h, d, e].wait_recv()
            c_bf[h, d, e] = push(
                h, at(first, step(1 - d)), at(second, step(1 - e)), e, second, e
            )
    for h, e in both:
        second, first = halves[h]
        c_b[h, "far", e, e].wait_recv()
        c_bf[h, "far", e] = push(h, at(first, 2), at(second, step(1 - e)), e, second, e)
    for h, d in both:
        c_b[h, "far", d, 1 - d].wait_recv()
    for copy in c_bf.values():
        copy.wait_recv()

    products(
        by_col, (slots + n_cols) // 2, lambda t, r: full[r], lambda t, r: tiles[t]
    )

    @pl.loop(0, 2 * SIDE)
    def _(o):
        for j in range(OWN):
            back[o // 2, lax.rem(o, 2), j] = held[by_col[3, o * OWN + j]]

    piece = [pl.ds(0, OWN // 2), pl.ds(OWN // 2, OWN // 2)]
    order = (2, 1, 3, 0)
    c_swap = [
        start(back.at[at("z", k), 1 - core], swap.at[i], mate) for i, k in enumerate(order)
    ]

    def add_mate(i):
        c_swap[i].wait_recv()
        index = at("z", order[i])

        @pl.loop(0, OWN)
        def _(t):
            value = back[index, core, t].astype(F32) + swap[i, t].astype(F32)
            total[i, t] = value
            half[i, t] = value.astype(BF16)

    add_mate(0)
    c_opp = [start(half.at[0, piece[d]], opp.at[d], peer("z", d)) for d in DIRS]
    c_plain = []
    for d in DIRS:
        add_mate(1 + d)
        c_plain.append(start(half.at[1 + d, piece[1 - d]], plain.at[d], peer("z", d)))
    add_mate(3)
    c_merged = []
    for d in DIRS:
        c_opp[d].wait_recv()

        @pl.loop(0, OWN // 2)
        def _(t):
            edge[d, t] = (total[1 + d, d * (OWN // 2) + t] + opp[d, t].astype(F32)).astype(BF16)

        c_merged.append(start(edge.at[d], merged.at[d], peer("z", d)))
    for d in DIRS:
        c_plain[1 - d].wait_recv()
        c_merged[d].wait_recv()
        for i in range(OWN // 2):
            t = d * (OWN // 2) + i
            value = total[3, t] + merged[d, i].astype(F32) + plain[1 - d, i].astype(F32)
            video_out[t] = blend(value, mass_video[t : t + 1], video_seeds[t : t + 1])
    copies.finish()


def sweep(by_row, by_col, v, tiles, in_row, in_col, audio_seeds, video_seeds):
    slots = tiles.shape[0]
    n_rows, n_cols = in_row.shape[0], in_col.shape[0]
    unit = (2, 2, SIDE, QUART, T, T)
    small = (2, 2, QUART, T, T)
    quad = (2, OWN // 2, T, T)
    count = 9 + 6 + 4 + 24 + 44 + 10
    scratch = [
        pltpu.VMEM((slots + 1, T, T), BF16),
        pltpu.VMEM(((slots + n_rows) // 2, T, T), BF16),
        pltpu.VMEM((n_cols, T, T), BF16),
        pltpu.VMEM((SIDE, SIDE, OWN, T, T), BF16),
        pltpu.VMEM((n_rows, T, T), BF16),
        pltpu.VMEM((SIDE, 2, OWN, T, T), BF16),
        pltpu.VMEM((T, T), F32),
        pltpu.VMEM((slots, T), F32),
        pltpu.VMEM((slots, T), F32),
        pltpu.VMEM((SIDE, SIDE, OWN, T), F32),
        pltpu.VMEM((SIDE, 2, OWN, T), F32),
        pltpu.VMEM(unit, BF16),
        pltpu.VMEM(unit, BF16),
        pltpu.VMEM(unit, BF16),
        pltpu.VMEM(unit, BF16),
        pltpu.VMEM(unit, F32),
        pltpu.VMEM(unit, BF16),
        pltpu.VMEM(small, BF16),
        pltpu.VMEM(small, BF16),
        pltpu.VMEM(small, BF16),
        pltpu.VMEM(small, BF16),
        pltpu.VMEM((SIDE, OWN, T), F32),
        pltpu.VMEM((SIDE, OWN, T), F32),
        pltpu.VMEM((SIDE, OWN, T), F32),
        pltpu.VMEM((2, SIDE, OWN, T), F32),
        pltpu.VMEM((OWN, T), F32),
        pltpu.VMEM((OWN, T), F32),
        pltpu.VMEM((2, OWN, T), F32),
        pltpu.VMEM((SIDE, OWN, T, T), BF16),
        pltpu.VMEM((SIDE, OWN, T, T), F32),
        pltpu.VMEM((SIDE, OWN, T, T), BF16),
        pltpu.VMEM(quad, BF16),
        pltpu.VMEM(quad, BF16),
        pltpu.VMEM(quad, BF16),
        pltpu.VMEM(quad, BF16),
        pltpu.VMEM((SIDE, OWN, T), F32),
        pltpu.VMEM((SIDE, OWN, T), F32),
        pltpu.VMEM((OWN, T), F32),
        pltpu.VMEM((OWN, T), F32),
        pltpu.VMEM((2, OWN, T), F32),
        pltpu.SemaphoreType.DMA((count,)),
        pltpu.SemaphoreType.DMA((count,)),
        pltpu.SemaphoreType.DMA((slots // CHUNK,)),
    ]
    return pl.pallas_call(
        sweep_kernel,
        in_specs=[SM, SM, VM, pl.BlockSpec(memory_space=pl.ANY), VM, VM, VM, VM],
        out_specs=[VM, VM],
        out_shape=[jax.ShapeDtypeStruct((OWN, T, T), F32)] * 2,
        scratch_shapes=scratch,
        compiler_params=pltpu.CompilerParams(
            collective_id=0, has_side_effects=True, vmem_limit_bytes=LIMIT
        ),
        name="sweep",
    )(by_row, by_col, v, tiles, in_row, in_col, audio_seeds, video_seeds)


def turn_kernel(a, b, a_out, b_out):
    for t in range(OWN):
        a_out[t] = a[t].T
        b_out[t] = b[t].T


def turn(a, b):
    return pl.pallas_call(
        turn_kernel,
        in_specs=[VM, VM],
        out_specs=[VM, VM],
        out_shape=[jax.ShapeDtypeStruct(a.shape, F32)] * 2,
        name="turn",
    )(a, b)


def body(video_scores_in, audio_seed, video_seed, tile_values, tile_rows, tile_cols, tile_count):
    n_rows, n_cols = SIDE * SIDE * OWN, 2 * SIDE * OWN
    by_row, by_col, in_row, in_col = plan(
        tile_count, tile_rows[0], tile_cols[0], n_rows, n_cols
    )
    audio, video = sweep(
        by_row,
        by_col,
        video_scores_in.reshape(OWN, T, T),
        tile_values[0, 0],
        in_row,
        in_col,
        audio_seed.reshape(OWN, T),
        video_seed.reshape(OWN, T),
    )
    audio, video = turn(audio, video)
    return (audio.reshape(OWN * T, T), video.reshape(OWN * T, T))


def solution(mesh):
    in_specs = (
        P(("col", "row"), None),
        P(("row", "col")),
        P(("col", "row")),
        P("row", "col", None, None, None),
        P("row", "col", None),
        P("row", "col", None),
        P("row", "col"),
    )
    out_specs = (P(("row", "col"), None), P(("col", "row"), None))
    return jax.shard_map(body, mesh=mesh, in_specs=in_specs, out_specs=out_specs, check_vma=False)
```

```python
import jax
import jax.numpy as jnp
from jax import lax
from jax.experimental import pallas as pl
from jax.experimental.pallas import tpu as pltpu
from jax.sharding import PartitionSpec as P

MESH = pl.DeviceIdType.MESH
F32, BF16 = jnp.float32, jnp.bfloat16
VM = pl.BlockSpec(memory_space=pltpu.VMEM)
SIDE = 4
OWN = 8
QUART = OWN // 4
T = 128
CHUNK = 32
UNROLL = 16
LIMIT = 67043328
DIRS = (0, 1)
REL = (2, 1, 3, 0)


def step(d):
    return 1 if d == 0 else SIDE - 1


class Copies:
    def __init__(self, send, recv):
        self.send, self.recv, self.used, self.open = send, recv, 0, []

    def slot(self):
        self.used += 1
        return self.used - 1

    def start(self, slot, src, dst, to):
        copy = pltpu.make_async_remote_copy(
            src_ref=src,
            dst_ref=dst,
            send_sem=self.send.at[slot],
            recv_sem=self.recv.at[slot],
            device_id=to,
            device_id_type=MESH,
        )
        copy.start()
        self.open.append(copy)
        return copy

    def finish(self):
        for copy in self.open:
            copy.wait_send()


def greet(peers):
    barrier = pltpu.get_barrier_semaphore()
    for peer in peers:
        pl.semaphore_signal(barrier, inc=1, device_id=peer, device_id_type=MESH)
    pl.semaphore_wait(barrier, len(peers))


def sort_slots(count, rows, cols, by_row, by_col, in_row, in_col):
    slots = rows.shape[1]
    wide = by_row.shape[1]
    lane = lax.broadcasted_iota(jnp.int32, (1, slots), 1)
    live = lane < count[0, 0]
    before = (
        lax.broadcasted_iota(jnp.int32, (slots, slots), 0)
        < lax.broadcasted_iota(jnp.int32, (slots, slots), 1)
    ).astype(BF16)
    below = (
        lax.broadcasted_iota(jnp.int32, (T, T), 0) > lax.broadcasted_iota(jnp.int32, (T, T), 1)
    ).astype(F32)

    def one(key, other, member, index):
        key = jnp.where(live, key, 1023)
        hit = (lax.broadcasted_iota(jnp.int32, (T, slots), 0) == key).astype(F32)
        member[...] = hit[: member.shape[0]].astype(BF16)
        rank = jnp.dot(hit.astype(BF16), before, preferred_element_type=F32)
        rank = jnp.sum(hit * rank, axis=0, keepdims=True)
        size = jnp.sum(hit, axis=1, keepdims=True)
        pairs = jnp.broadcast_to(jnp.floor((size + 1.0) * 0.5), (T, T))
        base = jnp.dot(
            below, pairs, preferred_element_type=F32, precision=lax.Precision.HIGHEST
        )
        start = jnp.sum(hit * base[:, :1], axis=0, keepdims=True)
        place = jnp.where(live, 2.0 * start + rank, -1.0)
        place = jnp.broadcast_to(place, (T, slots)).T
        high = lane // T
        part = lax.broadcasted_iota(jnp.int32, (8, slots), 0)
        facts = jnp.where(part == 0, high, lane - high * T)
        facts = jnp.where(part == 2, other, facts)
        facts = jnp.where(part == 3, 1, facts)
        facts = jnp.where(part == 4, (rank == 0.0).astype(jnp.int32), facts)
        facts = facts.astype(F32).astype(BF16)
        last = jnp.maximum(base + pairs - 1.0, 0.0).T
        row = lax.broadcasted_iota(jnp.int32, (8, T), 0)
        for c in range(wide // T):
            spot = lax.broadcasted_iota(jnp.int32, (slots, T), 1) + c * T
            chosen = (place == spot.astype(F32)).astype(BF16)
            got = jnp.dot(facts, chosen, preferred_element_type=F32)
            tile = got[0:1] * T + got[1:2] + slots * (1.0 - got[3:4])
            value = jnp.where(row == 0, tile, got[2:3])
            value = jnp.where(row == 2, 1.0 - got[4:5], value)
            value = jnp.where(row == 3, last[:8], value)
            index[:, c * T : (c + 1) * T] = value.astype(jnp.int32)

    one(rows[...], cols[...], in_row, by_row)
    one(cols[...], rows[...], in_col, by_col)


def plan_kernel(count_in, rows_in, cols_in, *refs):
    outs, count, rows, cols, found, sems = refs[:4], refs[4], refs[5], refs[6], refs[7:11], refs[11]
    pairs = [(count_in, count), (rows_in, rows), (cols_in, cols), *zip(found, outs)]
    moves = [pltpu.make_async_copy(a, b, sems.at[i]) for i, (a, b) in enumerate(pairs)]
    for move in moves[:3]:
        move.start()
    for move in moves[:3]:
        move.wait()
    sort_slots(count, rows, cols, *found)
    for move in moves[3:]:
        move.start()
    for move in moves[3:]:
        move.wait()


def plan(count, rows, cols, n_rows, n_cols):
    slots = rows.shape[1]
    wide = slots + n_rows
    anywhere = pl.BlockSpec(memory_space=pl.ANY)
    hbm = pl.BlockSpec(memory_space=pltpu.HBM)
    kinds = [
        ((8, wide), jnp.int32), ((8, wide), jnp.int32), ((n_rows, slots), BF16), ((n_cols, slots), BF16)
    ]
    return pl.pallas_call(
        plan_kernel,
        in_specs=[anywhere] * 3,
        out_specs=[hbm] * 4,
        out_shape=[jax.ShapeDtypeStruct(*kind) for kind in kinds],
        scratch_shapes=[
            pltpu.SMEM((1, 1), jnp.int32),
            pltpu.VMEM((1, slots), jnp.int32),
            pltpu.VMEM((1, slots), jnp.int32),
            *[pltpu.VMEM(*kind) for kind in kinds],
            pltpu.SemaphoreType.DMA((7,)),
        ],
        compiler_params=pltpu.CompilerParams(vmem_limit_bytes=60 * 1024 * 1024),
        name="plan",
    )(count, rows, cols)


def blend(total, mass, seeds):
    labels = (lax.broadcasted_iota(jnp.int32, total.shape, 0) == seeds).astype(F32)
    return total * (0.75 / jnp.sqrt(mass)) + 0.25 * labels


def sweep_kernel(
    by_row_in, by_col_in, in_row_in, in_col_in, v_in, tiles_in, audio_seeds_in, video_seeds_in,
    audio_out, video_out,
    tiles, held, panel, part, full, back, acc, row_sums, col_sums, mass_in, mass_col,
    by_row, by_col, in_row, in_col,
    v, audio_seeds, video_seeds, audio, video,
    opp1, plain1, merged1, edge1, half1, sum1, own1, opp2, plain2, merged2, edge2,
    mass_far, mass_edge, mass_sum, mass_hop, mass_far2, mass_edge2, mass_hop2,
    swap, total, half, opp, plain, merged, edge,
    r_swap, r_tot, r_far, r_edge, r_hop,
    send, recv, load, aux,
):
    slots = tiles_in.shape[0]
    n_chunks = slots // CHUNK
    n_cols = panel.shape[0]
    row_id, col_id = lax.axis_index("row"), lax.axis_index("col")
    core = lax.rem(row_id, 2)
    pos = {"y": col_id // SIDE, "x": lax.rem(col_id, SIDE), "z": row_id // 2}
    y, x, z = pos["y"], pos["x"], pos["z"]

    def at(axis, k):
        return lax.rem(pos[axis] + k, SIDE)

    def peer(axis, d):
        if axis == "y":
            return {"col": at("y", step(d)) * SIDE + x}
        if axis == "x":
            return {"col": y * SIDE + at("x", step(d))}
        return {"row": at("z", step(d)) * 2 + core}

    mate = {"row": z * 2 + 1 - core}
    copies = Copies(send, recv)

    def start(src, dst, to):
        return copies.start(copies.slot(), src, dst, to)

    def local(src, dst, slot):
        copy = pltpu.make_async_copy(src, dst, aux.at[slot])
        copy.start()
        return copy

    v_load = local(v_in, v, 0)
    index_loads = [local(by_row_in, by_row, 1), local(by_col_in, by_col, 2)]
    member_loads = [local(in_row_in, in_row, 3), local(in_col_in, in_col, 6)]
    seed_loads = [local(audio_seeds_in, audio_seeds, 4), local(video_seeds_in, video_seeds, 5)]
    loads = []
    for i in range(n_chunks):
        span = pl.ds(i * CHUNK, CHUNK)
        copy = pltpu.make_async_copy(tiles_in.at[span], tiles.at[span], load.at[i])
        copy.start()
        loads.append(copy)
    tiles[slots] = jnp.zeros((T, T), BF16)

    v_load.wait()
    panel[pl.ds(row_id * OWN, OWN)] = v[...].astype(BF16)
    greet([peer(axis, d) for axis in "xyz" for d in DIRS] + [mate])

    def push_video(index, first, size, to):
        ref = panel.at[pl.ds(index * OWN + first, size)]
        return start(ref, ref, to)

    def tile_sums(chunks):
        for i in chunks:
            loads[i].wait()

        @pl.loop(chunks[0], chunks[-1] + 1)
        def _(i):
            sums = lax.dot_general(
                jnp.ones((8, T), BF16),
                tiles[pl.ds(i * CHUNK, CHUNK)].reshape(CHUNK * T, T),
                (((1,), (1,)), ((), ())),
                preferred_element_type=F32,
            )
            for s in range(CHUNK):
                row_sums[pl.ds(i * CHUNK + s, 1)] = sums[0:1, s * T : (s + 1) * T]
                col_sums[pl.ds(i * CHUNK + s, 1)] = jnp.sum(
                    tiles[i * CHUNK + s].astype(F32), axis=0, keepdims=True
                )

    cut = (n_chunks * 7 // 20, n_chunks * 14 // 20)
    hop = [push_video(row_id, 0, OWN, peer("z", d)) for d in DIRS]
    mates = [push_video(row_id, 0, OWN, mate)]
    tile_sums(range(0, cut[0]))
    far = []
    for d in DIRS:
        index = at("z", step(1 - d)) * 2 + core
        hop[d].wait_recv()
        far.append(push_video(index, d * OWN // 2, OWN // 2, peer("z", d)))
        mates.append(push_video(index, 0, OWN, mate))
    tile_sums(range(cut[0], cut[1]))
    for d in DIRS:
        far[d].wait_recv()
        mates.append(push_video(at("z", 2) * 2 + core, d * OWN // 2, OWN // 2, mate))
    tile_sums(range(cut[1], n_chunks))

    def gathered(member, sums):
        value = sums[pl.ds(0, slots)]
        upper = value.astype(BF16)
        lower = (value - upper.astype(F32)).astype(BF16)
        return jnp.dot(member[...], upper, preferred_element_type=F32) + jnp.dot(
            member[...], lower, preferred_element_type=F32
        )

    for copy in member_loads:
        copy.wait()
    mass_in[...] = gathered(in_row, row_sums).reshape(mass_in.shape)
    mass_col[...] = gathered(in_col, col_sums).reshape(mass_col.shape)

    c_far = start(mass_in.at[:, at("x", 2)], mass_far, peer("x", 0))
    c_hop = start(mass_in.at[:, at("x", 3)], mass_hop.at[1], peer("x", 1))
    r_mate = start(mass_col.at[:, 1 - core], r_swap, mate)
    for copy in index_loads:
        copy.wait()
    for copy in mates:
        copy.wait_recv()

    def products(index, pairs, left, right, between=()):
        acc[...] = jnp.zeros_like(acc)
        steps, done = pairs // UNROLL, 0
        for n, act in enumerate(between):
            until = steps * (n + 1) // (len(between) + 1)
            some_products(index, done, until, left, right)
            act()
            done = until
        some_products(index, done, steps, left, right)

    def some_products(index, first, last, left, right):
        @pl.loop(first, last)
        def _(i):
            prods = []
            for u in range(UNROLL):
                g = (i * UNROLL + u) * 2
                a, b = (index[0, g], index[1, g]), (index[0, g + 1], index[1, g + 1])
                prods.append(
                    jnp.dot(
                        jnp.concatenate([left(*a), left(*b)], axis=1),
                        jnp.concatenate([right(*a), right(*b)], axis=0),
                        preferred_element_type=F32,
                    )
                )
            value = acc[...]
            for u in range(UNROLL):
                g = i * UNROLL + u
                value = value * index[2, g * 2].astype(F32) + prods[u]
                held[g] = value.astype(BF16)
            acc[...] = value

    moves = {"far": c_far, "hop": c_hop}

    def mass_1():
        moves["far"].wait_recv()
        mass_edge[...] = mass_far[...] + mass_in[:, at("x", 1)]
        moves["merge"] = start(mass_edge, mass_hop.at[0], peer("x", 0))
        r_mate.wait_recv()
        r_tot[...] = mass_col[:, core] + r_swap[...]
        moves["r_far"] = start(r_tot.at[at("z", 2)], r_far, peer("z", 0))
        moves["r_hop"] = start(r_tot.at[at("z", 3)], r_hop.at[1], peer("z", 1))

    def mass_2():
        moves["hop"].wait_recv()
        moves["merge"].wait_recv()
        mass_sum[...] = mass_in[:, x] + mass_hop[0] + mass_hop[1]
        moves["far"] = start(mass_sum.at[at("y", 2)], mass_far2, peer("y", 0))
        moves["hop"] = start(mass_sum.at[at("y", 3)], mass_hop2.at[1], peer("y", 1))
        moves["r_far"].wait_recv()
        r_edge[...] = r_far[...] + r_tot[at("z", 1)]
        moves["r_merge"] = start(r_edge, r_hop.at[0], peer("z", 0))

    def mass_3():
        moves["far"].wait_recv()
        mass_edge2[...] = mass_far2[...] + mass_sum[at("y", 1)]
        moves["merge"] = start(mass_edge2, mass_hop2.at[0], peer("y", 0))

    products(
        by_row,
        held.shape[0],
        lambda t, c: tiles[t],
        lambda t, c: panel[c],
        (mass_1, mass_2, mass_3),
    )

    @pl.loop(0, SIDE * SIDE)
    def _(o):
        for j in range(OWN):
            part[o // SIDE, lax.rem(o, SIDE), j] = held[by_row[3, o * OWN + j]]

    halves = (("x", "y"), ("y", "x"))

    def tiles_of(h, d):
        return pl.ds((2 * h + d) * QUART, QUART)

    both = [(h, d) for d in DIRS for h in (0, 1)]

    def cell(h, place, i, d):
        k = at(halves[h][1], REL[i])
        return part.at[k, place, tiles_of(h, d)] if h == 0 else part.at[place, k, tiles_of(h, d)]

    c_opp, c_plain, c_merged = {}, {}, {}

    def send_plain(i):
        for h, d in both:
            axis = halves[h][0]
            c_plain[h, d, i] = start(
                cell(h, at(axis, step(d)), i, 1 - d), plain1.at[h, d, i], peer(axis, d)
            )

    for i in range(SIDE):
        for h, d in both:
            axis = halves[h][0]
            c_opp[h, d, i] = start(cell(h, at(axis, 2), i, d), opp1.at[h, d, i], peer(axis, d))
    send_plain(0)
    for i in range(SIDE):
        for h, d in both:
            axis = halves[h][0]
            c_opp[h, d, i].wait_recv()
            mine = cell(h, at(axis, step(d)), i, d)
            edge1[h, d, i] = (mine[...].astype(F32) + opp1[h, d, i].astype(F32)).astype(BF16)
            c_merged[h, d, i] = start(edge1.at[h, d, i], merged1.at[h, d, i], peer(axis, d))
        if i + 1 < SIDE:
            send_plain(i + 1)

    def first_sum(h, d, i):
        c_plain[h, 1 - d, i].wait_recv()
        c_merged[h, d, i].wait_recv()
        mine = cell(h, pos[halves[h][0]], i, d)
        return (
            mine[...].astype(F32)
            + merged1[h, d, i].astype(F32)
            + plain1[h, 1 - d, i].astype(F32)
        )

    for h, d in both:
        half1[h, d, 0] = first_sum(h, d, 0).astype(BF16)
        axis = halves[h][1]
        c_opp[h, d] = start(half1.at[h, d, 0], opp2.at[h, d], peer(axis, d))
    for e in DIRS:
        for h, d in both:
            value = first_sum(h, d, 1 + e)
            if d == e:
                sum1[h, d] = value
            else:
                half1[h, d, 1] = value.astype(BF16)
                c_plain[h, e] = start(
                    half1.at[h, d, 1], plain2.at[h, e], peer(halves[h][1], e)
                )
    for h, d in both:
        c_opp[h, d].wait_recv()
        edge2[h, d] = (sum1[h, d] + opp2[h, d].astype(F32)).astype(BF16)
        c_merged[h, d] = start(edge2.at[h, d], merged2.at[h, d], peer(halves[h][1], d))
    for h, d in both:
        own1[h, d] = first_sum(h, d, 3)

    moves["hop"].wait_recv()
    moves["merge"].wait_recv()
    mass = mass_sum[y] + mass_hop2[0] + mass_hop2[1]
    moves["r_hop"].wait_recv()
    moves["r_merge"].wait_recv()
    mass_video = r_tot[z] + r_hop[0] + r_hop[1]
    for copy in seed_loads:
        copy.wait()

    def spot(h, k, u):
        return (k * SIDE + u) * OWN if h == 0 else (u * SIDE + k) * OWN

    for h, d in both:
        c_plain[h, 1 - d].wait_recv()
        c_merged[h, d].wait_recv()
        for i in range(QUART):
            t = (2 * h + d) * QUART + i
            value = (
                own1[h, d, i]
                + merged2[h, d, i].astype(F32)
                + plain2[h, 1 - d, i].astype(F32)
            )
            scores = blend(value.T, mass[t : t + 1], audio_seeds[t : t + 1])
            audio[t] = scores
            full[col_id * OWN + t] = scores.astype(BF16)

    def push(h, k, u, d, axis, way):
        if d is None:
            span = pl.ds(spot(h, k, u) + 2 * h * QUART, 2 * QUART)
        else:
            span = pl.ds(spot(h, k, u) + (2 * h + d) * QUART, QUART)
        ref = full.at[span]
        return start(ref, ref, peer(axis, way))

    audio_store = local(audio, audio_out, 7)
    c_a, c_af, c_b, c_bf = {}, {}, {}, {}
    for h in (0, 1):
        second, first = halves[h]
        for d in DIRS:
            c_a[h, d] = push(h, pos[first], pos[second], None, first, d)
    for h in (0, 1):
        second, first = halves[h]
        for d in DIRS:
            c_b[h, "own", d] = push(h, pos[first], pos[second], None, second, d)
    for h, d in both:
        second, first = halves[h]
        c_a[h, d].wait_recv()
        k = at(first, step(1 - d))
        c_af[h, d] = push(h, k, pos[second], d, first, d)
        for e in DIRS:
            c_b[h, d, e] = push(h, k, pos[second], None, second, e)
    for h, d in both:
        second, first = halves[h]
        c_b[h, "own", d].wait_recv()
        c_bf[h, "own", d] = push(h, pos[first], at(second, step(1 - d)), d, second, d)
    for h, d in both:
        second, first = halves[h]
        c_af[h, d].wait_recv()
        for e in DIRS:
            c_b[h, "far", d, e] = push(h, at(first, 2), pos[second], d, second, e)
    for h, e in both:
        second, first = halves[h]
        for d in DIRS:
            c_b[h, d, e].wait_recv()
            c_bf[h, d, e] = push(
                h, at(first, step(1 - d)), at(second, step(1 - e)), e, second, e
            )
    for h, e in both:
        second, first = halves[h]
        c_b[h, "far", e, e].wait_recv()
        c_bf[h, "far", e] = push(h, at(first, 2), at(second, step(1 - e)), e, second, e)
    for h, d in both:
        c_b[h, "far", d, 1 - d].wait_recv()
    for copy in c_bf.values():
        copy.wait_recv()

    products(
        by_col, (slots + n_cols) // 2, lambda t, r: full[r], lambda t, r: tiles[t]
    )

    @pl.loop(0, 2 * SIDE)
    def _(o):
        for j in range(OWN):
            back[o // 2, lax.rem(o, 2), j] = held[by_col[3, o * OWN + j]]

    piece = [pl.ds(0, OWN // 2), pl.ds(OWN // 2, OWN // 2)]
    order = (2, 1, 3, 0)
    c_swap = [
        start(back.at[at("z", k), 1 - core], swap.at[i], mate) for i, k in enumerate(order)
    ]

    def add_mate(i):
        c_swap[i].wait_recv()
        index = at("z", order[i])

        @pl.loop(0, OWN)
        def _(t):
            value = back[index, core, t].astype(F32) + swap[i, t].astype(F32)
            total[i, t] = value
            half[i, t] = value.astype(BF16)

    add_mate(0)
    c_opp = [start(half.at[0, piece[d]], opp.at[d], peer("z", d)) for d in DIRS]
    c_plain = []
    for d in DIRS:
        add_mate(1 + d)
        c_plain.append(start(half.at[1 + d, piece[1 - d]], plain.at[d], peer("z", d)))
    add_mate(3)
    c_merged = []
    for d in DIRS:
        c_opp[d].wait_recv()

        @pl.loop(0, OWN // 2)
        def _(t):
            edge[d, t] = (total[1 + d, d * (OWN // 2) + t] + opp[d, t].astype(F32)).astype(BF16)

        c_merged.append(start(edge.at[d], merged.at[d], peer("z", d)))
    for d in DIRS:
        c_plain[1 - d].wait_recv()
        c_merged[d].wait_recv()
        for i in range(OWN // 2):
            t = d * (OWN // 2) + i
            value = total[3, t] + merged[d, i].astype(F32) + plain[1 - d, i].astype(F32)
            video[t] = blend(value, mass_video[t : t + 1], video_seeds[t : t + 1])
    video_store = local(video, video_out, 8)
    audio_store.wait()
    video_store.wait()
    copies.finish()


def sweep(by_row, by_col, in_row, in_col, v, tiles, audio_seeds, video_seeds):
    slots = tiles.shape[0]
    n_rows, n_cols = SIDE * SIDE * OWN, 2 * SIDE * OWN
    wide = slots + n_rows
    unit = (2, 2, SIDE, QUART, T, T)
    small = (2, 2, QUART, T, T)
    quad = (2, OWN // 2, T, T)
    copies = 9 + 6 + 4 + 48 + 12 + 44 + 10
    scratch = [
        pltpu.VMEM((slots + 1, T, T), BF16),
        pltpu.VMEM((wide // 2, T, T), BF16),
        pltpu.VMEM((n_cols, T, T), BF16),
        pltpu.VMEM((SIDE, SIDE, OWN, T, T), BF16),
        pltpu.VMEM((n_rows, T, T), BF16),
        pltpu.VMEM((SIDE, 2, OWN, T, T), BF16),
        pltpu.VMEM((T, T), F32),
        pltpu.VMEM((slots, T), F32),
        pltpu.VMEM((slots, T), F32),
        pltpu.VMEM((SIDE, SIDE, OWN, T), F32),
        pltpu.VMEM((SIDE, 2, OWN, T), F32),
        pltpu.SMEM((8, wide), jnp.int32),
        pltpu.SMEM((8, wide), jnp.int32),
        pltpu.VMEM((n_rows, slots), BF16),
        pltpu.VMEM((n_cols, slots), BF16),
        pltpu.VMEM((OWN, T, T), F32),
        pltpu.VMEM((OWN, T), jnp.int32),
        pltpu.VMEM((OWN, T), jnp.int32),
        pltpu.VMEM((OWN, T, T), F32),
        pltpu.VMEM((OWN, T, T), F32),
        pltpu.VMEM(unit, BF16),
        pltpu.VMEM(unit, BF16),
        pltpu.VMEM(unit, BF16),
        pltpu.VMEM(unit, BF16),
        pltpu.VMEM((2, 2, 2, QUART, T, T), BF16),
        pltpu.VMEM(small, F32),
        pltpu.VMEM(small, F32),
        pltpu.VMEM(small, BF16),
        pltpu.VMEM(small, BF16),
        pltpu.VMEM(small, BF16),
        pltpu.VMEM(small, BF16),
        pltpu.VMEM((SIDE, OWN, T), F32),
        pltpu.VMEM((SIDE, OWN, T), F32),
        pltpu.VMEM((SIDE, OWN, T), F32),
        pltpu.VMEM((2, SIDE, OWN, T), F32),
        pltpu.VMEM((OWN, T), F32),
        pltpu.VMEM((OWN, T), F32),
        pltpu.VMEM((2, OWN, T), F32),
        pltpu.VMEM((SIDE, OWN, T, T), BF16),
        pltpu.VMEM((SIDE, OWN, T, T), F32),
        pltpu.VMEM((SIDE, OWN, T, T), BF16),
        pltpu.VMEM(quad, BF16),
        pltpu.VMEM(quad, BF16),
        pltpu.VMEM(quad, BF16),
        pltpu.VMEM(quad, BF16),
        pltpu.VMEM((SIDE, OWN, T), F32),
        pltpu.VMEM((SIDE, OWN, T), F32),
        pltpu.VMEM((OWN, T), F32),
        pltpu.VMEM((OWN, T), F32),
        pltpu.VMEM((2, OWN, T), F32),
        pltpu.SemaphoreType.DMA((copies,)),
        pltpu.SemaphoreType.DMA((copies,)),
        pltpu.SemaphoreType.DMA((slots // CHUNK,)),
        pltpu.SemaphoreType.DMA((9,)),
    ]
    anywhere = pl.BlockSpec(memory_space=pl.ANY)
    return pl.pallas_call(
        sweep_kernel,
        in_specs=[anywhere] * 8,
        out_specs=[anywhere] * 2,
        out_shape=[jax.ShapeDtypeStruct((OWN, T, T), F32)] * 2,
        scratch_shapes=scratch,
        compiler_params=pltpu.CompilerParams(
            collective_id=0, has_side_effects=True, vmem_limit_bytes=LIMIT
        ),
        name="sweep",
    )(by_row, by_col, in_row, in_col, v, tiles, audio_seeds, video_seeds)


def turn_kernel(a, b, a_out, b_out):
    for t in range(OWN):
        a_out[t] = a[t].T
        b_out[t] = b[t].T


def turn(a, b):
    return pl.pallas_call(
        turn_kernel,
        in_specs=[VM, VM],
        out_specs=[VM, VM],
        out_shape=[jax.ShapeDtypeStruct(a.shape, F32)] * 2,
        name="turn",
    )(a, b)


def body(video_scores_in, audio_seed, video_seed, tile_values, tile_rows, tile_cols, tile_count):
    n_rows, n_cols = SIDE * SIDE * OWN, 2 * SIDE * OWN
    by_row, by_col, in_row, in_col = plan(
        tile_count, tile_rows[0], tile_cols[0], n_rows, n_cols
    )
    audio, video = sweep(
        by_row,
        by_col,
        in_row,
        in_col,
        video_scores_in.reshape(OWN, T, T),
        tile_values[0, 0],
        audio_seed.reshape(OWN, T),
        video_seed.reshape(OWN, T),
    )
    audio, video = turn(audio, video)
    return (audio.reshape(OWN * T, T), video.reshape(OWN * T, T))


def solution(mesh):
    in_specs = (
        P(("col", "row"), None),
        P(("row", "col")),
        P(("col", "row")),
        P("row", "col", None, None, None),
        P("row", "col", None),
        P("row", "col", None),
        P("row", "col"),
    )
    out_specs = (P(("row", "col"), None), P(("col", "row"), None))
    return jax.shard_map(body, mesh=mesh, in_specs=in_specs, out_specs=out_specs, check_vma=False)
```

```python
import jax
import jax.numpy as jnp
from jax import lax
from jax.experimental import pallas as pl
from jax.experimental.pallas import tpu as pltpu
from jax.sharding import PartitionSpec as P

MESH = pl.DeviceIdType.MESH
F32, BF16 = jnp.float32, jnp.bfloat16
VM = pl.BlockSpec(memory_space=pltpu.VMEM)
SIDE = 4
OWN = 8
QUART = OWN // 4
T = 128
CHUNK = 32
AHEAD = 5
UNROLL = 32
LIMIT = 67043328
DIRS = (0, 1)
REL = (2, 1, 3, 0)


def step(d):
    return 1 if d == 0 else SIDE - 1


class Copies:
    def __init__(self, send, recv):
        self.send, self.recv, self.used, self.open = send, recv, 0, []

    def slot(self):
        self.used += 1
        return self.used - 1

    def start(self, slot, src, dst, to):
        copy = pltpu.make_async_remote_copy(
            src_ref=src,
            dst_ref=dst,
            send_sem=self.send.at[slot],
            recv_sem=self.recv.at[slot],
            device_id=to,
            device_id_type=MESH,
        )
        copy.start()
        self.open.append(copy)
        return copy

    def finish(self):
        for copy in self.open:
            copy.wait_send()


def greet(peers):
    barrier = pltpu.get_barrier_semaphore()
    for peer in peers:
        pl.semaphore_signal(barrier, inc=1, device_id=peer, device_id_type=MESH)
    return lambda: pl.semaphore_wait(barrier, len(peers))


def sort_slots(count, rows, cols, by_row, by_col, in_row, in_col):
    slots = rows.shape[1]
    wide = by_row.shape[1]
    lane = lax.broadcasted_iota(jnp.int32, (1, slots), 1)
    live = lane < count[0, 0]
    before = (
        lax.broadcasted_iota(jnp.int32, (slots, slots), 0)
        < lax.broadcasted_iota(jnp.int32, (slots, slots), 1)
    ).astype(BF16)
    below = (
        lax.broadcasted_iota(jnp.int32, (T, T), 0) > lax.broadcasted_iota(jnp.int32, (T, T), 1)
    ).astype(F32)

    def one(key, other, member, index):
        key = jnp.where(live, key, 1023)
        hit = (lax.broadcasted_iota(jnp.int32, (T, slots), 0) == key).astype(F32)
        member[...] = hit[: member.shape[0]].astype(BF16)
        rank = jnp.dot(hit.astype(BF16), before, preferred_element_type=F32)
        rank = jnp.sum(hit * rank, axis=0, keepdims=True)
        size = jnp.sum(hit, axis=1, keepdims=True)
        pairs = jnp.broadcast_to(jnp.floor((size + 1.0) * 0.5), (T, T))
        base = jnp.dot(
            below, pairs, preferred_element_type=F32, precision=lax.Precision.HIGHEST
        )
        start = jnp.sum(hit * base[:, :1], axis=0, keepdims=True)
        place = jnp.where(live, 2.0 * start + rank, -1.0)
        place = jnp.broadcast_to(place, (T, slots)).T
        high = lane // T
        part = lax.broadcasted_iota(jnp.int32, (8, slots), 0)
        facts = jnp.where(part == 0, high, lane - high * T)
        facts = jnp.where(part == 2, other, facts)
        facts = jnp.where(part == 3, 1, facts)
        facts = jnp.where(part == 4, (rank == 0.0).astype(jnp.int32), facts)
        facts = facts.astype(F32).astype(BF16)
        last = jnp.maximum(base + pairs - 1.0, 0.0).T
        row = lax.broadcasted_iota(jnp.int32, (8, T), 0)
        for c in range(wide // T):
            spot = lax.broadcasted_iota(jnp.int32, (slots, T), 1) + c * T
            chosen = (place == spot.astype(F32)).astype(BF16)
            got = jnp.dot(facts, chosen, preferred_element_type=F32)
            tile = got[0:1] * T + got[1:2] + slots * (1.0 - got[3:4])
            value = jnp.where(row == 0, tile, got[2:3])
            value = jnp.where(row == 2, 1.0 - got[4:5], value)
            value = jnp.where(row == 3, last[:8], value)
            index[:, c * T : (c + 1) * T] = value.astype(jnp.int32)

    one(rows[...], cols[...], in_row, by_row)
    one(cols[...], rows[...], in_col, by_col)


def plan_kernel(count_in, rows_in, cols_in, *refs):
    outs, count, rows, cols, found, sems = refs[:4], refs[4], refs[5], refs[6], refs[7:11], refs[11]
    pairs = [(count_in, count), (rows_in, rows), (cols_in, cols), *zip(found, outs)]
    moves = [pltpu.make_async_copy(a, b, sems.at[i]) for i, (a, b) in enumerate(pairs)]
    for move in moves[:3]:
        move.start()
    for move in moves[:3]:
        move.wait()
    sort_slots(count, rows, cols, *found)
    for move in moves[3:]:
        move.start()
    for move in moves[3:]:
        move.wait()


def plan(count, rows, cols, n_rows, n_cols):
    slots = rows.shape[1]
    wide = slots + n_rows
    anywhere = pl.BlockSpec(memory_space=pl.ANY)
    hbm = pl.BlockSpec(memory_space=pltpu.HBM)
    kinds = [
        ((8, wide), jnp.int32), ((8, wide), jnp.int32), ((n_rows, slots), BF16), ((n_cols, slots), BF16)
    ]
    return pl.pallas_call(
        plan_kernel,
        in_specs=[anywhere] * 3,
        out_specs=[hbm] * 4,
        out_shape=[jax.ShapeDtypeStruct(*kind) for kind in kinds],
        scratch_shapes=[
            pltpu.SMEM((1, 1), jnp.int32),
            pltpu.VMEM((1, slots), jnp.int32),
            pltpu.VMEM((1, slots), jnp.int32),
            *[pltpu.VMEM(*kind) for kind in kinds],
            pltpu.SemaphoreType.DMA((7,)),
        ],
        compiler_params=pltpu.CompilerParams(vmem_limit_bytes=60 * 1024 * 1024),
        name="plan",
    )(count, rows, cols)


def blend(total, mass, seeds):
    labels = (lax.broadcasted_iota(jnp.int32, total.shape, 0) == seeds).astype(F32)
    return total * (0.75 / jnp.sqrt(mass)) + 0.25 * labels


def sweep_kernel(
    by_row_in, by_col_in, in_row_in, in_col_in, v_in, tiles_in, audio_seeds_in, video_seeds_in,
    audio_out, video_out,
    tiles, held, panel, part, full, back, acc, row_sums, col_sums, mass_in, mass_col,
    by_row, by_col, in_row, in_col,
    v, audio_seeds, video_seeds, audio, video,
    opp1, plain1, merged1, edge1, half1, sum1, own1, opp2, plain2, merged2, edge2,
    mass_far, mass_edge, mass_sum, mass_hop, mass_far2, mass_edge2, mass_hop2,
    swap, total, half, opp, plain, merged, edge,
    r_swap, r_tot, r_far, r_edge, r_hop,
    send, recv, load, aux,
):
    slots = tiles_in.shape[0]
    n_chunks = slots // CHUNK
    n_cols = panel.shape[0]
    row_id, col_id = lax.axis_index("row"), lax.axis_index("col")
    core = lax.rem(row_id, 2)
    pos = {"y": col_id // SIDE, "x": lax.rem(col_id, SIDE), "z": row_id // 2}
    y, x, z = pos["y"], pos["x"], pos["z"]

    def at(axis, k):
        return lax.rem(pos[axis] + k, SIDE)

    def peer(axis, d):
        if axis == "y":
            return {"col": at("y", step(d)) * SIDE + x}
        if axis == "x":
            return {"col": y * SIDE + at("x", step(d))}
        return {"row": at("z", step(d)) * 2 + core}

    mate = {"row": z * 2 + 1 - core}
    copies = Copies(send, recv)

    def start(src, dst, to):
        return copies.start(copies.slot(), src, dst, to)

    def local(src, dst, slot):
        copy = pltpu.make_async_copy(src, dst, aux.at[slot])
        copy.start()
        return copy

    met = greet([peer(axis, d) for axis in "xyz" for d in DIRS] + [mate])
    v_load = local(v_in, v, 0)

    def chunk(i):
        span = pl.ds(i * CHUNK, CHUNK)
        return pltpu.make_async_copy(tiles_in.at[span], tiles.at[span], load.at[i])

    for i in range(AHEAD):
        chunk(i).start()
    index_loads = [local(by_row_in, by_row, 1), local(by_col_in, by_col, 2)]
    member_loads = [local(in_row_in, in_row, 3), local(in_col_in, in_col, 6)]
    seed_loads = [local(audio_seeds_in, audio_seeds, 4), local(video_seeds_in, video_seeds, 5)]
    tiles[slots] = jnp.zeros((T, T), BF16)

    v_load.wait()
    panel[pl.ds(row_id * OWN, OWN)] = v[...].astype(BF16)
    met()

    def push_video(index, d, to):
        ref = panel.at[pl.ds(index * OWN + d * (OWN // 2), OWN // 2)]
        return start(ref, ref, to)

    def tile_sums(first, last):
        @pl.loop(first, last)
        def _(i):
            @pl.when(i + AHEAD < n_chunks)
            def _():
                chunk(i + AHEAD).start()

            chunk(i).wait()
            sums = lax.dot_general(
                jnp.ones((8, T), BF16),
                tiles[pl.ds(i * CHUNK, CHUNK)].reshape(CHUNK * T, T),
                (((1,), (1,)), ((), ())),
                preferred_element_type=F32,
            )
            for s in range(CHUNK):
                row_sums[pl.ds(i * CHUNK + s, 1)] = sums[0:1, s * T : (s + 1) * T]
                col_sums[pl.ds(i * CHUNK + s, 1)] = jnp.sum(
                    tiles[i * CHUNK + s].astype(F32), axis=0, keepdims=True
                )

    near = [peer("z", d) for d in DIRS]
    origin = [at("z", step(1 - d)) * 2 + core for d in DIRS]
    early = [push_video(row_id, d, near[d]) for d in DIRS]
    late = [push_video(row_id, 1 - d, near[d]) for d in DIRS]
    mates = [push_video(row_id, d, mate) for d in DIRS]
    tile_sums(0, n_chunks // 2)
    far = []
    for d in DIRS:
        early[d].wait_recv()
        far.append(push_video(origin[d], d, near[d]))
        mates.append(push_video(origin[d], d, mate))
    tile_sums(n_chunks // 2, n_chunks)
    for d in DIRS:
        late[d].wait_recv()
        mates.append(push_video(origin[d], 1 - d, mate))

    def gathered(member, sums):
        value = sums[pl.ds(0, slots)]
        upper = value.astype(BF16)
        lower = (value - upper.astype(F32)).astype(BF16)
        return jnp.dot(member[...], upper, preferred_element_type=F32) + jnp.dot(
            member[...], lower, preferred_element_type=F32
        )

    for copy in member_loads:
        copy.wait()
    mass_in[...] = gathered(in_row, row_sums).reshape(mass_in.shape)
    mass_col[...] = gathered(in_col, col_sums).reshape(mass_col.shape)

    c_far = start(mass_in.at[:, at("x", 2)], mass_far, peer("x", 0))
    c_hop = start(mass_in.at[:, at("x", 3)], mass_hop.at[1], peer("x", 1))
    r_mate = start(mass_col.at[:, 1 - core], r_swap, mate)
    for d in DIRS:
        far[d].wait_recv()
        mates.append(push_video(at("z", 2) * 2 + core, d, mate))
    for copy in index_loads:
        copy.wait()
    for copy in mates:
        copy.wait_recv()

    def products(index, pairs, left, right, between=()):
        acc[...] = jnp.zeros_like(acc)
        steps, done = pairs // UNROLL, 0
        for n, act in enumerate(between):
            until = steps * (n + 1) // (len(between) + 1)
            some_products(index, done, until, left, right)
            act()
            done = until
        some_products(index, done, steps, left, right)

    def some_products(index, first, last, left, right):
        @pl.loop(first, last)
        def _(i):
            prods = []
            for u in range(UNROLL):
                g = (i * UNROLL + u) * 2
                a, b = (index[0, g], index[1, g]), (index[0, g + 1], index[1, g + 1])
                prods.append(
                    jnp.dot(
                        jnp.concatenate([left(*a), left(*b)], axis=1),
                        jnp.concatenate([right(*a), right(*b)], axis=0),
                        preferred_element_type=F32,
                    )
                )
            value = acc[...]
            for u in range(UNROLL):
                g = i * UNROLL + u
                value = value * index[2, g * 2].astype(F32) + prods[u]
                held[g] = value.astype(BF16)
            acc[...] = value

    moves = {"far": c_far, "hop": c_hop}

    def mass_1():
        moves["far"].wait_recv()
        mass_edge[...] = mass_far[...] + mass_in[:, at("x", 1)]
        moves["merge"] = start(mass_edge, mass_hop.at[0], peer("x", 0))
        r_mate.wait_recv()
        r_tot[...] = mass_col[:, core] + r_swap[...]
        moves["r_far"] = start(r_tot.at[at("z", 2)], r_far, peer("z", 0))
        moves["r_hop"] = start(r_tot.at[at("z", 3)], r_hop.at[1], peer("z", 1))

    def mass_2():
        moves["hop"].wait_recv()
        moves["merge"].wait_recv()
        mass_sum[...] = mass_in[:, x] + mass_hop[0] + mass_hop[1]
        moves["far"] = start(mass_sum.at[at("y", 2)], mass_far2, peer("y", 0))
        moves["hop"] = start(mass_sum.at[at("y", 3)], mass_hop2.at[1], peer("y", 1))
        moves["r_far"].wait_recv()
        r_edge[...] = r_far[...] + r_tot[at("z", 1)]
        moves["r_merge"] = start(r_edge, r_hop.at[0], peer("z", 0))

    def mass_3():
        moves["far"].wait_recv()
        mass_edge2[...] = mass_far2[...] + mass_sum[at("y", 1)]
        moves["merge"] = start(mass_edge2, mass_hop2.at[0], peer("y", 0))

    products(
        by_row,
        held.shape[0],
        lambda t, c: tiles[t],
        lambda t, c: panel[c],
        (mass_1,),
    )
    mass_2()

    @pl.loop(0, SIDE * SIDE)
    def _(o):
        for j in range(OWN):
            part[o // SIDE, lax.rem(o, SIDE), j] = held[by_row[3, o * OWN + j]]

    halves = (("x", "y"), ("y", "x"))

    def tiles_of(h, d):
        return pl.ds((2 * h + d) * QUART, QUART)

    both = [(h, d) for d in DIRS for h in (0, 1)]

    def cell(h, place, i, d):
        k = at(halves[h][1], REL[i])
        return part.at[k, place, tiles_of(h, d)] if h == 0 else part.at[place, k, tiles_of(h, d)]

    c_opp, c_plain, c_merged = {}, {}, {}

    def send_plain(i):
        for h, d in both:
            axis = halves[h][0]
            c_plain[h, d, i] = start(
                cell(h, at(axis, step(d)), i, 1 - d), plain1.at[h, d, i], peer(axis, d)
            )

    for i in range(SIDE):
        for h, d in both:
            axis = halves[h][0]
            c_opp[h, d, i] = start(cell(h, at(axis, 2), i, d), opp1.at[h, d, i], peer(axis, d))
    send_plain(0)
    mass_3()
    for i in range(SIDE):
        for h, d in both:
            axis = halves[h][0]
            c_opp[h, d, i].wait_recv()
            mine = cell(h, at(axis, step(d)), i, d)
            edge1[h, d, i] = (mine[...].astype(F32) + opp1[h, d, i].astype(F32)).astype(BF16)
            c_merged[h, d, i] = start(edge1.at[h, d, i], merged1.at[h, d, i], peer(axis, d))
        if i + 1 < SIDE:
            send_plain(i + 1)

    def first_sum(h, d, i):
        c_plain[h, 1 - d, i].wait_recv()
        c_merged[h, d, i].wait_recv()
        mine = cell(h, pos[halves[h][0]], i, d)
        return (
            mine[...].astype(F32)
            + merged1[h, d, i].astype(F32)
            + plain1[h, 1 - d, i].astype(F32)
        )

    for h, d in both:
        half1[h, d, 0] = first_sum(h, d, 0).astype(BF16)
        axis = halves[h][1]
        c_opp[h, d] = start(half1.at[h, d, 0], opp2.at[h, d], peer(axis, d))
    for e in DIRS:
        for h, d in both:
            value = first_sum(h, d, 1 + e)
            if d == e:
                sum1[h, d] = value
            else:
                half1[h, d, 1] = value.astype(BF16)
                c_plain[h, e] = start(
                    half1.at[h, d, 1], plain2.at[h, e], peer(halves[h][1], e)
                )
    for h, d in both:
        c_opp[h, d].wait_recv()
        edge2[h, d] = (sum1[h, d] + opp2[h, d].astype(F32)).astype(BF16)
        c_merged[h, d] = start(edge2.at[h, d], merged2.at[h, d], peer(halves[h][1], d))
    for h, d in both:
        own1[h, d] = first_sum(h, d, 3)

    moves["hop"].wait_recv()
    moves["merge"].wait_recv()
    mass = mass_sum[y] + mass_hop2[0] + mass_hop2[1]
    moves["r_hop"].wait_recv()
    moves["r_merge"].wait_recv()
    mass_video = r_tot[z] + r_hop[0] + r_hop[1]
    for copy in seed_loads:
        copy.wait()

    def spot(h, k, u):
        return (k * SIDE + u) * OWN if h == 0 else (u * SIDE + k) * OWN

    for h, d in both:
        c_plain[h, 1 - d].wait_recv()
        c_merged[h, d].wait_recv()
        for i in range(QUART):
            t = (2 * h + d) * QUART + i
            value = (
                own1[h, d, i]
                + merged2[h, d, i].astype(F32)
                + plain2[h, 1 - d, i].astype(F32)
            )
            scores = blend(value.T, mass[t : t + 1], audio_seeds[t : t + 1])
            audio[t] = scores
            full[col_id * OWN + t] = scores.astype(BF16)

    def push(h, k, u, d, axis, way):
        if d is None:
            span = pl.ds(spot(h, k, u) + 2 * h * QUART, 2 * QUART)
        else:
            span = pl.ds(spot(h, k, u) + (2 * h + d) * QUART, QUART)
        ref = full.at[span]
        return start(ref, ref, peer(axis, way))

    audio_store = local(audio, audio_out, 7)
    c_a, c_af, c_b, c_bf = {}, {}, {}, {}
    for h in (0, 1):
        second, first = halves[h]
        for d in DIRS:
            c_a[h, d] = push(h, pos[first], pos[second], None, first, d)
    for h in (0, 1):
        second, first = halves[h]
        for d in DIRS:
            c_b[h, "own", d] = push(h, pos[first], pos[second], None, second, d)
    for h, d in both:
        second, first = halves[h]
        c_a[h, d].wait_recv()
        k = at(first, step(1 - d))
        c_af[h, d] = push(h, k, pos[second], d, first, d)
        for e in DIRS:
            c_b[h, d, e] = push(h, k, pos[second], None, second, e)
    for h, d in both:
        second, first = halves[h]
        c_b[h, "own", d].wait_recv()
        c_bf[h, "own", d] = push(h, pos[first], at(second, step(1 - d)), d, second, d)
    for h, d in both:
        second, first = halves[h]
        c_af[h, d].wait_recv()
        for e in DIRS:
            c_b[h, "far", d, e] = push(h, at(first, 2), pos[second], d, second, e)
    for h, e in both:
        second, first = halves[h]
        for d in DIRS:
            c_b[h, d, e].wait_recv()
            c_bf[h, d, e] = push(
                h, at(first, step(1 - d)), at(second, step(1 - e)), e, second, e
            )
    for h, e in both:
        second, first = halves[h]
        c_b[h, "far", e, e].wait_recv()
        c_bf[h, "far", e] = push(h, at(first, 2), at(second, step(1 - e)), e, second, e)
    for h, d in both:
        c_b[h, "far", d, 1 - d].wait_recv()
    for copy in c_bf.values():
        copy.wait_recv()

    products(
        by_col, (slots + n_cols) // 2, lambda t, r: full[r], lambda t, r: tiles[t]
    )

    @pl.loop(0, 2 * SIDE)
    def _(o):
        for j in range(OWN):
            back[o // 2, lax.rem(o, 2), j] = held[by_col[3, o * OWN + j]]

    piece = [pl.ds(0, OWN // 2), pl.ds(OWN // 2, OWN // 2)]
    order = (2, 1, 3, 0)
    c_swap = [
        start(back.at[at("z", k), 1 - core], swap.at[i], mate) for i, k in enumerate(order)
    ]

    def add_mate(i):
        c_swap[i].wait_recv()
        index = at("z", order[i])

        @pl.loop(0, OWN)
        def _(t):
            value = back[index, core, t].astype(F32) + swap[i, t].astype(F32)
            total[i, t] = value
            half[i, t] = value.astype(BF16)

    add_mate(0)
    c_opp = [start(half.at[0, piece[d]], opp.at[d], peer("z", d)) for d in DIRS]
    c_plain = []
    for d in DIRS:
        add_mate(1 + d)
        c_plain.append(start(half.at[1 + d, piece[1 - d]], plain.at[d], peer("z", d)))
    add_mate(3)
    c_merged = []
    for d in DIRS:
        c_opp[d].wait_recv()

        @pl.loop(0, OWN // 2)
        def _(t):
            edge[d, t] = (total[1 + d, d * (OWN // 2) + t] + opp[d, t].astype(F32)).astype(BF16)

        c_merged.append(start(edge.at[d], merged.at[d], peer("z", d)))
    for d in DIRS:
        c_plain[1 - d].wait_recv()
        c_merged[d].wait_recv()
        for i in range(OWN // 2):
            t = d * (OWN // 2) + i
            value = total[3, t] + merged[d, i].astype(F32) + plain[1 - d, i].astype(F32)
            video[t] = blend(value, mass_video[t : t + 1], video_seeds[t : t + 1])
    video_store = local(video, video_out, 8)
    audio_store.wait()
    video_store.wait()
    copies.finish()


def sweep(by_row, by_col, in_row, in_col, v, tiles, audio_seeds, video_seeds):
    slots = tiles.shape[0]
    n_rows, n_cols = SIDE * SIDE * OWN, 2 * SIDE * OWN
    wide = slots + n_rows
    unit = (2, 2, SIDE, QUART, T, T)
    small = (2, 2, QUART, T, T)
    quad = (2, OWN // 2, T, T)
    copies = 14 + 6 + 4 + 48 + 12 + 44 + 10
    scratch = [
        pltpu.VMEM((slots + 1, T, T), BF16),
        pltpu.VMEM((wide // 2, T, T), BF16),
        pltpu.VMEM((n_cols, T, T), BF16),
        pltpu.VMEM((SIDE, SIDE, OWN, T, T), BF16),
        pltpu.VMEM((n_rows, T, T), BF16),
        pltpu.VMEM((SIDE, 2, OWN, T, T), BF16),
        pltpu.VMEM((T, T), F32),
        pltpu.VMEM((slots, T), F32),
        pltpu.VMEM((slots, T), F32),
        pltpu.VMEM((SIDE, SIDE, OWN, T), F32),
        pltpu.VMEM((SIDE, 2, OWN, T), F32),
        pltpu.SMEM((8, wide), jnp.int32),
        pltpu.SMEM((8, wide), jnp.int32),
        pltpu.VMEM((n_rows, slots), BF16),
        pltpu.VMEM((n_cols, slots), BF16),
        pltpu.VMEM((OWN, T, T), F32),
        pltpu.VMEM((OWN, T), jnp.int32),
        pltpu.VMEM((OWN, T), jnp.int32),
        pltpu.VMEM((OWN, T, T), F32),
        pltpu.VMEM((OWN, T, T), F32),
        pltpu.VMEM(unit, BF16),
        pltpu.VMEM(unit, BF16),
        pltpu.VMEM(unit, BF16),
        pltpu.VMEM(unit, BF16),
        pltpu.VMEM((2, 2, 2, QUART, T, T), BF16),
        pltpu.VMEM(small, F32),
        pltpu.VMEM(small, F32),
        pltpu.VMEM(small, BF16),
        pltpu.VMEM(small, BF16),
        pltpu.VMEM(small, BF16),
        pltpu.VMEM(small, BF16),
        pltpu.VMEM((SIDE, OWN, T), F32),
        pltpu.VMEM((SIDE, OWN, T), F32),
        pltpu.VMEM((SIDE, OWN, T), F32),
        pltpu.VMEM((2, SIDE, OWN, T), F32),
        pltpu.VMEM((OWN, T), F32),
        pltpu.VMEM((OWN, T), F32),
        pltpu.VMEM((2, OWN, T), F32),
        pltpu.VMEM((SIDE, OWN, T, T), BF16),
        pltpu.VMEM((SIDE, OWN, T, T), F32),
        pltpu.VMEM((SIDE, OWN, T, T), BF16),
        pltpu.VMEM(quad, BF16),
        pltpu.VMEM(quad, BF16),
        pltpu.VMEM(quad, BF16),
        pltpu.VMEM(quad, BF16),
        pltpu.VMEM((SIDE, OWN, T), F32),
        pltpu.VMEM((SIDE, OWN, T), F32),
        pltpu.VMEM((OWN, T), F32),
        pltpu.VMEM((OWN, T), F32),
        pltpu.VMEM((2, OWN, T), F32),
        pltpu.SemaphoreType.DMA((copies,)),
        pltpu.SemaphoreType.DMA((copies,)),
        pltpu.SemaphoreType.DMA((slots // CHUNK,)),
        pltpu.SemaphoreType.DMA((9,)),
    ]
    anywhere = pl.BlockSpec(memory_space=pl.ANY)
    return pl.pallas_call(
        sweep_kernel,
        in_specs=[anywhere] * 8,
        out_specs=[anywhere] * 2,
        out_shape=[jax.ShapeDtypeStruct((OWN, T, T), F32)] * 2,
        scratch_shapes=scratch,
        compiler_params=pltpu.CompilerParams(
            collective_id=0, has_side_effects=True, vmem_limit_bytes=LIMIT
        ),
        name="sweep",
    )(by_row, by_col, in_row, in_col, v, tiles, audio_seeds, video_seeds)


def turn_kernel(a, b, a_out, b_out, before, after, load, store):
    half = OWN // 2
    moves = []
    for i, (src, dst) in enumerate(((a, a_out), (b, b_out))):
        for k in range(2):
            span, n = pl.ds(k * half, half), 2 * i + k
            moves.append(
                (
                    pltpu.make_async_copy(src.at[span], before.at[n], load.at[n]),
                    pltpu.make_async_copy(after.at[n], dst.at[span], store.at[n]),
                )
            )
            moves[-1][0].start()
    for n, (come, go) in enumerate(moves):
        come.wait()
        for t in range(half):
            after[n, t] = before[n, t].T
        go.start()
    for _, go in moves:
        go.wait()


def turn(a, b):
    anywhere = pl.BlockSpec(memory_space=pl.ANY)
    return pl.pallas_call(
        turn_kernel,
        in_specs=[anywhere] * 2,
        out_specs=[anywhere] * 2,
        out_shape=[jax.ShapeDtypeStruct(a.shape, F32)] * 2,
        scratch_shapes=[
            pltpu.VMEM((4, OWN // 2, T, T), F32),
            pltpu.VMEM((4, OWN // 2, T, T), F32),
            pltpu.SemaphoreType.DMA((4,)),
            pltpu.SemaphoreType.DMA((4,)),
        ],
        compiler_params=pltpu.CompilerParams(vmem_limit_bytes=LIMIT),
        name="turn",
    )(a, b)


def body(video_scores_in, audio_seed, video_seed, tile_values, tile_rows, tile_cols, tile_count):
    n_rows, n_cols = SIDE * SIDE * OWN, 2 * SIDE * OWN
    by_row, by_col, in_row, in_col = plan(
        tile_count, tile_rows[0], tile_cols[0], n_rows, n_cols
    )
    audio, video = sweep(
        by_row,
        by_col,
        in_row,
        in_col,
        video_scores_in.reshape(OWN, T, T),
        tile_values[0, 0],
        audio_seed.reshape(OWN, T),
        video_seed.reshape(OWN, T),
    )
    audio, video = turn(audio, video)
    return (audio.reshape(OWN * T, T), video.reshape(OWN * T, T))


def solution(mesh):
    in_specs = (
        P(("col", "row"), None),
        P(("row", "col")),
        P(("col", "row")),
        P("row", "col", None, None, None),
        P("row", "col", None),
        P("row", "col", None),
        P("row", "col"),
    )
    out_specs = (P(("row", "col"), None), P(("col", "row"), None))
    return jax.shard_map(body, mesh=mesh, in_specs=in_specs, out_specs=out_specs, check_vma=False)
```
